32 devices in a mesh: group: 2 (over y), seq: 16 (over z, x, core).
Axes of the slice: x: 2, y: 2, z: 4, core: 2. Of those that a mesh axis runs over, the one named last changes fastest.
Arguments:
- queries: bfloat16 [4096, 4096], P(('group', 'seq')), parts along dimension 0, may hold values from -64 to 64
- key_vectors: bfloat16 [4096, 1024], P(('group', 'seq')), parts along dimension 0, may hold values from -2 to 2
- value_vectors: bfloat16 [4096, 1024], P(('group', 'seq')), parts along dimension 0, may hold values from -6 to 6
- grad_output: bfloat16 [4096, 4096], P(('group', 'seq')), parts along dimension 0, may hold values from -6 to 6
- document_ids: int32 [4096], P('group'), parts along dimension 0, may hold values from 0 to 3, never falling along the last dimension, each value on 1 to 1024 neighbouring positions
Outputs:
- attention_out: bfloat16 [4096, 4096], P(('group', 'seq')), parts along dimension 0
- grad_queries: bfloat16 [4096, 4096], P(('group', 'seq')), parts along dimension 0
- grad_keys: bfloat16 [4096, 1024], P(('group', 'seq')), parts along dimension 0
- grad_values: bfloat16 [4096, 1024], P(('group', 'seq')), parts along dimension 0
The draws below stay inside these ranges and needn't reach their ends.
There are 2 independent parts, one for each index of `group`. The reference program is written for one: setup_inputs(seed, part) draws one part's arguments, and reference() takes and returns one part's arrays. A program takes and returns all parts, laid end to end along the dimension named above; each array names one. Nothing has to cross between parts.
Inputs may be any that keep to these rules, and one draw needn't show every extreme that they name: `document_ids`: document numbers never fall along positions; each document covers 1 to 1024 consecutive positions and one covers exactly 1024.
All inputs are finite; a program needn't handle non-finite values.
Results may differ from the reference program's by a relative error of at most 0.015.
Values may be sent and summed in bfloat16 or wider, within the bound.
No kernel may reach another device: no remote copies, remote signals or barrier semaphores. Data moves between devices by JAX's collectives and lax.ppermute only.
A program may use at most 128 MiB of HBM per device.

```python
import math
import jax
import jax.numpy as jnp
import numpy as np
from jax import lax

H = 32
KV = 8
HD = 128
TOK_DEV = 128
MOST = 1024
TOKENS = 2048
DOCS = 4
N_SEQ = 16


def paired_draw(key):
    folded = jax.random.fold_in(key, 11)
    query_seed, key_seed = jax.random.split(folded, 2)
    query_table = jax.random.truncated_normal(query_seed, -6.0, 6.0, (TOKENS, H * HD), jnp.float32)
    key_table = jax.random.truncated_normal(key_seed, -2.0, 2.0, (TOKENS, KV * HD), jnp.float32)
    return (query_table, key_table)


def draw_queries(key, part):
    return paired_draw(key)[0].astype(jnp.bfloat16)


def draw_key_vectors(key, part):
    return paired_draw(key)[1].astype(jnp.bfloat16)


def steps_of(key, dims, shards, smallest, top_value):
    loudness, own = 1.0, jax.random.fold_in(key, 6)
    for axis_at, parts in shards:
        draws = jnp.exp(jax.random.uniform(jax.random.fold_in(own, axis_at), (parts,), jnp.float32, smallest / len(shards), top_value / len(shards)))
        loudness = loudness * jnp.repeat(draws, dims[axis_at] // parts).reshape([-1 if axis == axis_at else 1 for axis in range(len(dims))])
    return loudness


def split_up(number_of, total, reach, lean):
    portions = [(1 << 20) // math.isqrt(standing ** lean) + 1 for standing in range(2, number_of + 1)]
    rest, counts = total - reach - (number_of - 1), [1] * (number_of - 1)
    while rest > 0:
        free = [i for i in range(number_of - 1) if counts[i] < reach]
        pool, remaining = sum([portions[i] for i in free]), rest
        for i in free:
            more = min(reach - counts[i], max(1, remaining * portions[i] // pool), rest)
            counts[i] = counts[i] + more
            rest = rest - more
    return np.array([reach] + counts)


def ragged(rng, number_of, total, bound, slope):
    if number_of == 2:
        one = jax.random.randint(rng, (), max(1, total - bound), min(bound, total - 1) + 1)
        return jnp.stack([one, total - one])
    tallies = jnp.asarray(split_up(number_of, total, bound, slope), jnp.int32)
    pairs = (number_of - 1) // 2
    source_of, sink = tallies[1:1 + 2 * pairs:2], tallies[2:2 + 2 * pairs:2]
    slack = jnp.minimum(source_of - 1, bound - sink)
    moved = jax.random.randint(jax.random.fold_in(rng, 1), (pairs,), 0, 1 << 20) % (slack + 1)
    tallies = tallies.at[1:1 + 2 * pairs:2].set(source_of - moved).at[2:2 + 2 * pairs:2].set(sink + moved)
    return tallies[jax.random.permutation(jax.random.fold_in(rng, 2), number_of)]


def gaussian(key, dims, deviation, reach, shards=(), kind=jnp.bfloat16):
    values = jax.random.normal(key, dims, jnp.float32) * deviation
    if len(shards) > 0:
        values = steps_of(key, dims, shards, -0.22, 0.18) * values
    return jnp.clip(values, min=-reach, max=reach).astype(kind)


def setup_inputs(seed: int = 0, part: int = 0) -> dict:
    arg_keys = jax.random.split(jax.random.key(seed), 6)
    own_keys = jax.random.split(jax.random.fold_in(arg_keys[5], part), 6)
    queries = draw_queries(jax.random.fold_in(jax.random.fold_in(arg_keys[5], part), 71), part)
    key_vectors = draw_key_vectors(jax.random.fold_in(jax.random.fold_in(arg_keys[5], part), 71), part)
    value_vectors = gaussian(own_keys[2], (TOKENS, KV * HD), 1.0, 6.0, ((0, 16),))
    grad_output = gaussian(own_keys[3], (TOKENS, H * HD), 1.0, 6.0, ((0, 16),))
    document_ids = jnp.searchsorted(jnp.cumsum(ragged(own_keys[4], DOCS, TOKENS, MOST, 1)), jnp.arange(TOKENS), side="right").astype(jnp.int32)
    return dict(queries=queries, key_vectors=key_vectors, value_vectors=value_vectors, grad_output=grad_output, document_ids=document_ids)


def attend_block(query_block, grad_block, key_block, value_block, allowed):
    score_scale = 1.0 / math.sqrt(query_block.shape[-1])
    scores = jnp.einsum('qgd,kd->gqk', query_block.astype(jnp.float32), key_block.astype(jnp.float32)) * score_scale
    scores = jnp.where(allowed[None], scores, -1e+30)
    row_max = lax.optimization_barrier(jnp.max(scores, axis=-1, keepdims=True))
    weights = jnp.exp(scores - row_max)
    softmax = weights / lax.optimization_barrier(jnp.sum(weights, axis=-1, keepdims=True))
    probs_low = softmax.astype(jnp.bfloat16)
    output = jnp.einsum('gqk,kd->qgd', probs_low.astype(jnp.float32), value_block.astype(jnp.float32)).astype(jnp.bfloat16)
    row_delta = lax.optimization_barrier(jnp.sum(grad_block.astype(jnp.float32) * output.astype(jnp.float32), axis=-1))
    grad_probs = jnp.einsum('qgd,kd->gqk', grad_block.astype(jnp.float32), value_block.astype(jnp.float32))
    grad_scores = (softmax * (grad_probs - jnp.transpose(row_delta)[:, :, None])).astype(jnp.bfloat16)
    grad_query = (jnp.einsum('gqk,kd->qgd', grad_scores.astype(jnp.float32), key_block.astype(jnp.float32)) * score_scale).astype(jnp.bfloat16)
    grad_key = jnp.einsum('gqk,qgd->kd', grad_scores.astype(jnp.float32), query_block.astype(jnp.float32)) * score_scale
    grad_value = jnp.einsum('gqk,qgd->kd', probs_low.astype(jnp.float32), grad_block.astype(jnp.float32))
    return (output, grad_query, grad_key, grad_value)

def reference(queries, key_vectors, value_vectors, grad_output, document_ids):
    group = H // KV
    block_rows = min(512, TOK_DEV * KV)
    blocks = TOKENS // block_rows

    def to_order(tensor):
        return tensor.reshape(N_SEQ, TOK_DEV, -1).transpose(1, 0, 2).reshape(TOKENS, -1)

    def from_order(tensor):
        return tensor.reshape(TOK_DEV, N_SEQ, -1).transpose(1, 0, 2).reshape(TOKENS, -1)
    query_all = to_order(queries).reshape(TOKENS, KV, group, HD).transpose(1, 0, 2, 3)
    grad_all = to_order(grad_output).reshape(TOKENS, KV, group, HD).transpose(1, 0, 2, 3)
    key_all = to_order(key_vectors).reshape(TOKENS, KV, HD).transpose(1, 0, 2)
    value_all = to_order(value_vectors).reshape(TOKENS, KV, HD).transpose(1, 0, 2)
    key_all = jnp.concatenate([jnp.zeros((KV, MOST, HD), key_all.dtype), key_all], axis=1)
    value_all = jnp.concatenate([jnp.zeros((KV, MOST, HD), value_all.dtype), value_all], axis=1)
    padded_ids = jnp.concatenate([jnp.full((MOST,), -1, jnp.int32), document_ids.astype(jnp.int32)])
    column_index = jnp.arange(block_rows + MOST, dtype=jnp.int32)[None, :]
    row_index = jnp.arange(block_rows, dtype=jnp.int32)[:, None]

    def one_head(operands):
        query_head, grad_head, key_head, value_head = operands

        def one_block(totals, block_index):
            key_grad, value_grad = totals
            offset = (block_index * block_rows).astype(jnp.int32)
            query_block = lax.dynamic_slice_in_dim(query_head, offset, block_rows, 0)
            grad_block = lax.dynamic_slice_in_dim(grad_head, offset, block_rows, 0)
            key_block = lax.dynamic_slice_in_dim(key_head, offset, block_rows + MOST, 0)
            value_block = lax.dynamic_slice_in_dim(value_head, offset, block_rows + MOST, 0)
            row_ids = lax.dynamic_slice_in_dim(document_ids.astype(jnp.int32), offset, block_rows)
            column_ids = lax.dynamic_slice_in_dim(padded_ids, offset, block_rows + MOST)
            allowed = (row_ids[:, None] == column_ids[None, :]) & (column_index <= row_index + MOST)
            output, grad_query, grad_key, grad_value = attend_block(query_block, grad_block, key_block, value_block, allowed)
            key_grad = lax.dynamic_update_slice_in_dim(key_grad, lax.dynamic_slice_in_dim(key_grad, offset, block_rows + MOST, 0) + grad_key, offset, 0)
            value_grad = lax.dynamic_update_slice_in_dim(value_grad, lax.dynamic_slice_in_dim(value_grad, offset, block_rows + MOST, 0) + grad_value, offset, 0)
            return ((key_grad, value_grad), (output, grad_query))
        zeros_init = jnp.zeros((TOKENS + MOST, HD), jnp.float32)
        (key_grad, value_grad), (outputs, grad_queries) = lax.scan(one_block, (zeros_init, zeros_init), jnp.arange(blocks, dtype=jnp.int32))
        return (outputs, grad_queries, key_grad[MOST:].astype(jnp.bfloat16), value_grad[MOST:].astype(jnp.bfloat16))
    outputs, grad_query_all, grad_key_all, grad_value_all = lax.map(one_head, (query_all, grad_all, key_all, value_all))
    attention_out = from_order(outputs.transpose(1, 2, 0, 3, 4).reshape(TOKENS, H * HD))
    grad_queries = from_order(grad_query_all.transpose(1, 2, 0, 3, 4).reshape(TOKENS, H * HD))
    grad_keys = from_order(grad_key_all.transpose(1, 0, 2).reshape(TOKENS, KV * HD))
    grad_values = from_order(grad_value_all.transpose(1, 0, 2).reshape(TOKENS, KV * HD))
    return (attention_out, grad_queries, grad_keys, grad_values)
```

```python
import functools
import math

import jax
import jax.numpy as jnp
from jax import lax
from jax.experimental import pallas as pl
from jax.experimental.pallas import tpu as pltpu
from jax.sharding import PartitionSpec as P

H = 32
KV = 8
HD = 128
MOST = 1024
GROUP = H // KV
QR = 16
KR = 16
F32 = jnp.float32
BF16 = jnp.bfloat16
SCALE = 1.0 / math.sqrt(HD)
EXP2_SCALE = SCALE * math.log2(math.e)


def attend_kernel(heads, lanes, depth, start_ref, begin_ref, place_ref, key_place_ref, *refs):
    refs = list(refs)
    take = lambda count: [refs.pop(0) for _ in range(count)]
    query_refs, kv_refs = take(lanes), take(depth)
    out_refs, grad_refs = take(lanes), take(depth)
    key_turned, value_turned, key_sum, value_sum, score_ref, out_sum, query_sum = refs
    rows = query_refs[0].shape[1]
    key_tiles, query_tiles = rows // KR, rows // QR
    tile = depth * lanes * KR
    span = lanes * GROUP * QR

    def keys_of(which, head, step):
        at = pl.ds(pl.multiple_of(step * KR, KR), KR)
        columns = slice(head * HD, (head + 1) * HD)
        return jnp.concatenate(
            [ref[:, which, at, columns].reshape(lanes * KR, HD) for ref in kv_refs], axis=0
        )

    def queries_of(which, head, step):
        at = pl.ds(pl.multiple_of(step * QR, QR), QR)
        return jnp.concatenate(
            [
                ref[which, at, (head * GROUP + j) * HD : (head * GROUP + j + 1) * HD]
                for j in range(GROUP)
                for ref in query_refs
            ],
            axis=0,
        )

    def put_queries(which, head, step, value):
        at = pl.ds(pl.multiple_of(step * QR, QR), QR)
        for j in range(GROUP):
            for lane, ref in enumerate(out_refs):
                low = (j * lanes + lane) * QR
                ref[which, at, (head * GROUP + j) * HD : (head * GROUP + j + 1) * HD] = value[
                    low : low + QR
                ]

    for head in range(heads):

        @pl.loop(0, key_tiles)
        def _(step):
            key_turned[step] = keys_of(0, head, step).T
            value_turned[step] = keys_of(1, head, step).T
            key_sum[step] = jnp.zeros((tile, HD), F32)
            value_sum[step] = jnp.zeros((tile, HD), F32)

        @pl.loop(0, query_tiles)
        def _(turn):
            query, grad = queries_of(0, head, turn), queries_of(1, head, turn)
            query_t, grad_t = query.T, grad.T
            first = start_ref[turn]
            last = (turn + 1) * (QR // KR)
            begin, place = begin_ref[turn], place_ref[turn]

            def score(step, top):
                base = step * (tile // depth // lanes) * depth * lanes
                value = jnp.dot(keys_of(0, head, step), query_t, preferred_element_type=F32)
                key_place = jnp.concatenate([key_place_ref[...]] * (span // 128), axis=1)
                allowed = (key_place <= place - base) & (key_place >= begin - base)
                value = jnp.where(allowed, value, -1e30)
                score_ref[step - first] = value
                return jnp.maximum(top, value.reshape(tile // 8, 8, span).max(axis=0))

            top = lax.fori_loop(first, last, score, jnp.full((8, span), -1e30, F32))
            top = jnp.max(top, axis=0, keepdims=True)
            out_sum[...] = jnp.zeros((HD, span), F32)

            def weigh(step, total):
                weight = jnp.exp2((score_ref[step - first] - top) * EXP2_SCALE)
                score_ref[step - first] = weight
                out_sum[...] += jnp.dot(
                    value_turned[step], weight.astype(BF16), preferred_element_type=F32
                )
                return total + weight.reshape(tile // 8, 8, span).sum(axis=0)

            total = lax.fori_loop(first, last, weigh, jnp.zeros((8, span), F32))
            inverse = 1.0 / jnp.sum(total, axis=0, keepdims=True)
            out_t = (out_sum[...] * inverse).astype(BF16).astype(F32)
            delta = jnp.sum(out_t * grad_t.astype(F32), axis=0, keepdims=True)
            put_queries(0, head, turn, out_t.T.astype(BF16))
            query_sum[...] = jnp.zeros((HD, span), F32)

            def back(step, carry):
                prob = score_ref[step - first] * inverse
                value_sum[step] += jnp.dot(prob.astype(BF16), grad, preferred_element_type=F32)
                grad_prob = jnp.dot(keys_of(1, head, step), grad_t, preferred_element_type=F32)
                grad_score = (prob * (grad_prob - delta)).astype(BF16)
                key_sum[step] += jnp.dot(grad_score, query, preferred_element_type=F32)
                query_sum[...] += jnp.dot(
                    key_turned[step], grad_score, preferred_element_type=F32
                )
                return carry

            lax.fori_loop(first, last, back, 0)
            put_queries(1, head, turn, (query_sum[...] * SCALE).T.astype(BF16))

        @pl.loop(0, key_tiles)
        def _(step):
            at = pl.ds(pl.multiple_of(step * KR, KR), KR)
            columns = slice(head * HD, (head + 1) * HD)
            for which, total, factor in ((0, key_sum, SCALE), (1, value_sum, 1.0)):
                for k, ref in enumerate(grad_refs):
                    low = k * lanes * KR
                    part = total[step, low : low + lanes * KR, :] * factor
                    ref[:, which, at, columns] = part.astype(ref.dtype).reshape(lanes, KR, HD)


def attend(query_parts, kv_parts, starts, begins, places, key_places):
    lanes, depth = len(query_parts), len(kv_parts)
    _, rows, columns = query_parts[0].shape
    heads = columns // (GROUP * HD)
    tile, span = depth * lanes * KR, lanes * GROUP * QR
    key_tiles = rows // KR
    reach = QR // KR + -(-(MOST - 1) // tile)
    vmem = pl.BlockSpec(memory_space=pltpu.VMEM)
    pairs = heads * GROUP * rows * lanes * 640
    return pl.pallas_call(
        functools.partial(attend_kernel, heads, lanes, depth),
        out_shape=[jax.ShapeDtypeStruct(part.shape, BF16) for part in query_parts]
        + [
            jax.ShapeDtypeStruct(part.shape, F32 if k == 0 else BF16)
            for k, part in enumerate(kv_parts)
        ],
        in_specs=[pl.BlockSpec(memory_space=pltpu.SMEM)] + [vmem] * (3 + lanes + depth),
        out_specs=[vmem] * (lanes + depth),
        scratch_shapes=[
            pltpu.VMEM((key_tiles, HD, tile), BF16),
            pltpu.VMEM((key_tiles, HD, tile), BF16),
            pltpu.VMEM((key_tiles, tile, HD), F32),
            pltpu.VMEM((key_tiles, tile, HD), F32),
            pltpu.VMEM((min(reach, key_tiles), tile, span), F32),
            pltpu.VMEM((HD, span), F32),
            pltpu.VMEM((HD, span), F32),
        ],
        compiler_params=pltpu.CompilerParams(vmem_limit_bytes=60 << 20),
        cost_estimate=pl.CostEstimate(
            flops=10 * HD * pairs, bytes_accessed=8 << 20, transcendentals=pairs
        ),
    )(starts, begins, places, key_places, *query_parts, *kv_parts)


def swapped(tensor, mask):
    devices = lax.axis_size("seq")
    return lax.ppermute(tensor, "seq", [(i, i ^ mask) for i in range(devices)])


def on_device(queries, key_vectors, value_vectors, grad_output, document_ids):
    devices = lax.axis_size("seq")
    position = lax.axis_index("seq")
    rows = queries.shape[0]
    lanes = min(KV, devices // 4)
    depth = devices // lanes
    lane = position % lanes
    above = position - lane
    wide, narrow = H * HD // lanes, KV * HD // lanes

    def cut(tensor, mask, width):
        return lax.dynamic_slice_in_dim(tensor, (lane ^ mask) * width, width, 1)

    def kv_cut(mask):
        return jnp.stack([cut(key_vectors, mask, narrow), cut(value_vectors, mask, narrow)])

    def query_cut(mask):
        return jnp.stack([cut(queries, mask, wide), cut(grad_output, mask, wide)])

    kv_own = jnp.stack(
        [kv_cut(0)] + [swapped(kv_cut(mask), mask) for mask in range(1, lanes)]
    )
    kv_parts = [kv_own] + [swapped(kv_own, k * lanes) for k in range(1, depth)]
    query_parts = [query_cut(0)] + [swapped(query_cut(mask), mask) for mask in range(1, lanes)]

    ids = document_ids.reshape(rows, devices)
    lane_masks = jnp.arange(lanes, dtype=jnp.int32)
    mine = above + (lane ^ lane_masks)
    column = jnp.arange(devices, dtype=jnp.int32)
    own_ids = jnp.sum(
        jnp.where(column[None, None, :] == mine[:, None, None], ids[None], 0), axis=-1
    )
    begin = jnp.sum(
        (document_ids[None, None, :] < own_ids[:, :, None]).astype(jnp.int32), axis=-1
    )
    place = jnp.arange(rows, dtype=jnp.int32)[None, :] * devices + mine[:, None]

    def tiled(values):
        parts = values.reshape(lanes, rows // QR, QR).transpose(1, 0, 2)
        parts = parts.reshape(rows // QR, 1, lanes * QR)
        return jnp.tile(parts, (1, 1, GROUP))

    begins, places = tiled(begin), tiled(place)
    starts = jnp.min(begins, axis=(1, 2)) // (KR * devices)
    chunk = (jnp.arange(depth, dtype=jnp.int32) * lanes) ^ above
    key_place = (
        jnp.arange(KR, dtype=jnp.int32)[None, None, :] * devices
        + chunk[:, None, None]
        + (lane ^ lane_masks)[None, :, None]
    ).reshape(depth * lanes * KR, 1)
    key_places = jnp.broadcast_to(key_place, (depth * lanes * KR, 128))

    results = attend(query_parts, kv_parts, starts, begins, places, key_places)
    out_parts, grad_parts = results[:lanes], results[lanes:]
    out_back = [out_parts[0]] + [swapped(out_parts[mask], mask) for mask in range(1, lanes)]
    total = grad_parts[0]
    for k in range(1, depth):
        total = total + swapped(grad_parts[k], k * lanes).astype(F32)
    total = total.astype(BF16)
    kv_back = [total[0]] + [swapped(total[mask], mask) for mask in range(1, lanes)]

    def joined(parts, which, width):
        whole = jnp.zeros((rows, lanes * width), BF16)
        for mask, part in enumerate(parts):
            whole = lax.dynamic_update_slice_in_dim(whole, part[which], (lane ^ mask) * width, 1)
        return whole

    return (
        joined(out_back, 0, wide),
        joined(out_back, 1, wide),
        joined(kv_back, 0, narrow),
        joined(kv_back, 1, narrow),
    )


def solution(mesh):
    placed = P(("group", "seq"), None)
    return jax.shard_map(
        on_device,
        mesh=mesh,
        in_specs=(placed, placed, placed, placed, P("group")),
        out_specs=(placed, placed, placed, placed),
        check_vma=False,
    )
```

```python
import functools
import math

import jax
import jax.numpy as jnp
from jax import lax
from jax.experimental import pallas as pl
from jax.experimental.pallas import tpu as pltpu
from jax.sharding import PartitionSpec as P

H = 32
KV = 8
HD = 128
MOST = 1024
GROUP = H // KV
KR = 16
F32 = jnp.float32
BF16 = jnp.bfloat16
SCALE = 1.0 / math.sqrt(HD)
EXP2_SCALE = SCALE * math.log2(math.e)


def query_rows(lanes):
    return max(16, 128 // lanes)


def attend_kernel(head, lanes, depth, start_ref, begin_ref, place_ref, key_place_ref, *refs):
    refs = list(refs)
    take = lambda count: [refs.pop(0) for _ in range(count)]
    query_refs, kv_refs = take(lanes), take(depth)
    out_refs, grad_refs = take(lanes), take(depth)
    key_turned, value_turned, key_sum, value_sum, score_ref, out_sum, query_sum = refs
    rows = query_refs[0].shape[1]
    turn_rows = query_rows(lanes)
    key_tiles, query_tiles = rows // KR, rows // turn_rows
    tile = depth * lanes * KR
    span = lanes * GROUP * turn_rows

    def keys_of(which, step):
        at = pl.ds(pl.multiple_of(step * KR, KR), KR)
        return jnp.concatenate(
            [ref[:, which, at, :].reshape(lanes * KR, HD) for ref in kv_refs], axis=0
        )

    def queries_of(which, step):
        at = pl.ds(pl.multiple_of(step * turn_rows, turn_rows), turn_rows)
        return jnp.concatenate(
            [
                ref[which, at, (head * GROUP + j) * HD : (head * GROUP + j + 1) * HD]
                for j in range(GROUP)
                for ref in query_refs
            ],
            axis=0,
        )

    def put_queries(which, step, value):
        at = pl.ds(pl.multiple_of(step * turn_rows, turn_rows), turn_rows)
        for j in range(GROUP):
            for lane, ref in enumerate(out_refs):
                low = (j * lanes + lane) * turn_rows
                ref[which, at, j * HD : (j + 1) * HD] = value[low : low + turn_rows]

    @pl.loop(0, key_tiles)
    def _(step):
        key_turned[step] = keys_of(0, step).T
        value_turned[step] = keys_of(1, step).T
        key_sum[step] = jnp.zeros((tile, HD), F32)
        value_sum[step] = jnp.zeros((tile, HD), F32)

    @pl.loop(0, query_tiles)
    def _(turn):
        query, grad = queries_of(0, turn), queries_of(1, turn)
        query_t, grad_t = query.T, grad.T
        first = start_ref[turn]
        last = (turn + 1) * (turn_rows // KR)
        begin, place = begin_ref[turn], place_ref[turn]

        def solve(count):
            tops = jnp.full((8, span), -1e30, F32)
            steps = [last - count + i for i in range(count)]
            key_place = jnp.concatenate([key_place_ref[...]] * (span // 128), axis=1)
            for i, step in enumerate(steps):
                base = step * tile
                value = jnp.dot(keys_of(0, step), query_t, preferred_element_type=F32)
                allowed = key_place >= begin - base
                if i >= count - turn_rows // KR:
                    allowed = allowed & (key_place <= place - base)
                value = jnp.where(allowed, value, -1e30)
                score_ref[i] = value
                tops = jnp.maximum(tops, value.reshape(tile // 8, 8, span).max(axis=0))
            top = jnp.max(tops, axis=0, keepdims=True) * EXP2_SCALE
            total = jnp.zeros((8, span), F32)
            out_t = jnp.zeros((HD, span), F32)
            for i, step in enumerate(steps):
                weight = jnp.exp2(score_ref[i] * EXP2_SCALE - top)
                score_ref[i] = weight
                out_t += jnp.dot(
                    value_turned[step], weight.astype(BF16), preferred_element_type=F32
                )
                total += weight.reshape(tile // 8, 8, span).sum(axis=0)
            inverse = 1.0 / jnp.sum(total, axis=0, keepdims=True)
            out_t = (out_t * inverse).astype(BF16).astype(F32)
            delta = jnp.sum(out_t * grad_t.astype(F32), axis=0, keepdims=True)
            put_queries(0, turn, out_t.T.astype(BF16))
            query_total = jnp.zeros((HD, span), F32)
            for i, step in enumerate(steps):
                prob = score_ref[i] * inverse
                value_sum[step] += jnp.dot(prob.astype(BF16), grad, preferred_element_type=F32)
                grad_prob = jnp.dot(keys_of(1, step), grad_t, preferred_element_type=F32)
                grad_score = (prob * (grad_prob - delta)).astype(BF16)
                key_sum[step] += jnp.dot(grad_score, query, preferred_element_type=F32)
                query_total += jnp.dot(
                    key_turned[step], grad_score, preferred_element_type=F32
                )
            put_queries(1, turn, (query_total * SCALE).T.astype(BF16))

        for count in range(1, score_ref.shape[0] + 1):

            @pl.when(last - first == count)
            def _():
                solve(count)

    @pl.loop(0, key_tiles)
    def _(step):
        at = pl.ds(pl.multiple_of(step * KR, KR), KR)
        for which, total, factor in ((0, key_sum, SCALE), (1, value_sum, 1.0)):
            for k, ref in enumerate(grad_refs):
                low = k * lanes * KR
                part = total[step, low : low + lanes * KR, :] * factor
                ref[:, which, at, :] = part.astype(ref.dtype).reshape(lanes, KR, HD)


def attend(head, query_parts, kv_parts, starts, begins, places, key_places):
    lanes, depth = len(query_parts), len(kv_parts)
    rows = query_parts[0].shape[1]
    turn_rows = query_rows(lanes)
    tile, span = depth * lanes * KR, lanes * GROUP * turn_rows
    key_tiles = rows // KR
    reach = turn_rows // KR + -(-(MOST - 1) // tile)
    vmem = pl.BlockSpec(memory_space=pltpu.VMEM)
    pairs = GROUP * rows * lanes * 640
    return pl.pallas_call(
        functools.partial(attend_kernel, head, lanes, depth),
        out_shape=[jax.ShapeDtypeStruct((2, rows, GROUP * HD), BF16)] * lanes
        + [
            jax.ShapeDtypeStruct(part.shape, F32 if k == 0 or (k == 2 and depth == 4) else BF16)
            for k, part in enumerate(kv_parts)
        ],
        in_specs=[pl.BlockSpec(memory_space=pltpu.SMEM)] + [vmem] * (3 + lanes + depth),
        out_specs=[vmem] * (lanes + depth),
        scratch_shapes=[
            pltpu.VMEM((key_tiles, HD, tile), BF16),
            pltpu.VMEM((key_tiles, HD, tile), BF16),
            pltpu.VMEM((key_tiles, tile, HD), F32),
            pltpu.VMEM((key_tiles, tile, HD), F32),
            pltpu.VMEM((min(reach, key_tiles), tile, span), F32),
            pltpu.VMEM((HD, span), F32),
            pltpu.VMEM((HD, span), F32),
        ],
        compiler_params=pltpu.CompilerParams(vmem_limit_bytes=(40 if depth == 4 else 62) << 20),
        cost_estimate=pl.CostEstimate(
            flops=10 * HD * pairs, bytes_accessed=8 << 20, transcendentals=pairs
        ),
    )(starts, begins, places, key_places, *query_parts, *kv_parts)


def moved(tensor, target):
    devices = lax.axis_size("seq")
    return lax.ppermute(tensor, "seq", [(i, target(i)) for i in range(devices)])


def swapped(tensor, mask):
    return moved(tensor, lambda i: i ^ mask)


def middle_swapped(tensor, lanes):
    return moved(tensor, lambda i: i if i // lanes in (0, 3) else i ^ (3 * lanes))


def gathered(own, lanes, depth, inner):
    if depth != 4:
        return [own] + [swapped(own, k * lanes) for k in range(1, depth)]
    two = swapped(own, 2 * lanes)
    one = swapped(own, lanes)
    three = middle_swapped(own, lanes)
    passed = swapped(two, lanes)
    return [own, one, two, jnp.where(inner, three, passed)]


def summed(parts, lanes, depth, inner):
    total = parts[0]
    if depth != 4:
        for k in range(1, depth):
            total = total + swapped(parts[k].astype(BF16), k * lanes).astype(F32)
        return total.astype(BF16)
    passed = swapped(parts[3], lanes)
    one = swapped(parts[1], lanes)
    three = middle_swapped(parts[3], lanes)
    two = (parts[2] + jnp.where(inner, passed.astype(F32), 0.0)).astype(BF16)
    two = swapped(two, 2 * lanes)
    total = total + one.astype(F32) + two.astype(F32)
    return (total + jnp.where(inner, three.astype(F32), 0.0)).astype(BF16)


def on_device(queries, key_vectors, value_vectors, grad_output, document_ids):
    devices = lax.axis_size("seq")
    position = lax.axis_index("seq")
    rows = queries.shape[0]
    lanes = min(KV, devices // 4)
    depth = devices // lanes
    lane = position % lanes
    above = position - lane
    level = position // lanes
    inner = (level > 0) & (level < depth - 1)
    heads = KV // lanes
    wide, narrow = H * HD // lanes, KV * HD // lanes

    def cut(tensor, mask, width):
        return lax.dynamic_slice_in_dim(tensor, (lane ^ mask) * width, width, 1)

    def kv_cut(mask):
        both = jnp.stack([cut(key_vectors, mask, narrow), cut(value_vectors, mask, narrow)])
        return jnp.stack([both[:, :, h * HD : (h + 1) * HD] for h in range(heads)])

    def query_cut(mask):
        return jnp.stack([cut(queries, mask, wide), cut(grad_output, mask, wide)])

    kv_lanes = [kv_cut(0)] + [swapped(kv_cut(mask), mask) for mask in range(1, lanes)]
    query_parts = [query_cut(0)] + [swapped(query_cut(mask), mask) for mask in range(1, lanes)]
    kv_parts = [
        gathered(jnp.stack([part[h] for part in kv_lanes]), lanes, depth, inner)
        for h in range(heads)
    ]

    ids = document_ids.reshape(rows, devices)
    lane_masks = jnp.arange(lanes, dtype=jnp.int32)
    mine = above + (lane ^ lane_masks)
    column = jnp.arange(devices, dtype=jnp.int32)
    own_ids = jnp.sum(
        jnp.where(column[None, None, :] == mine[:, None, None], ids[None], 0), axis=-1
    )
    begin = jnp.sum(
        (document_ids[None, None, :] < own_ids[:, :, None]).astype(jnp.int32), axis=-1
    )
    place = jnp.arange(rows, dtype=jnp.int32)[None, :] * devices + mine[:, None]

    turn_rows = query_rows(lanes)

    def tiled(values):
        parts = values.reshape(lanes, rows // turn_rows, turn_rows).transpose(1, 0, 2)
        parts = parts.reshape(rows // turn_rows, 1, lanes * turn_rows)
        return jnp.tile(parts, (1, 1, GROUP))

    begins, places = tiled(begin), tiled(place)
    starts = jnp.min(begins, axis=(1, 2)) // (KR * devices)
    chunk = (jnp.arange(depth, dtype=jnp.int32) * lanes) ^ above
    key_place = (
        jnp.arange(KR, dtype=jnp.int32)[None, None, :] * devices
        + chunk[:, None, None]
        + (lane ^ lane_masks)[None, :, None]
    ).reshape(depth * lanes * KR, 1)
    key_places = jnp.broadcast_to(key_place, (depth * lanes * KR, 128))

    wholes = [jnp.zeros((rows, H * HD), BF16) for _ in range(2)]
    kv_wholes = [jnp.zeros((rows, KV * HD), BF16) for _ in range(2)]
    for h in range(heads):
        results = attend(h, query_parts, kv_parts[h], starts, begins, places, key_places)
        out_parts, grad_parts = results[:lanes], results[lanes:]
        out_back = [out_parts[0]] + [swapped(out_parts[mask], mask) for mask in range(1, lanes)]
        total = summed(grad_parts, lanes, depth, inner)
        kv_back = [total[0]] + [swapped(total[mask], mask) for mask in range(1, lanes)]
        for which in range(2):
            for mask in range(lanes):
                owner = lane ^ mask
                wholes[which] = lax.dynamic_update_slice_in_dim(
                    wholes[which], out_back[mask][which], owner * wide + h * GROUP * HD, 1
                )
                kv_wholes[which] = lax.dynamic_update_slice_in_dim(
                    kv_wholes[which], kv_back[mask][which], owner * narrow + h * HD, 1
                )
    return (wholes[0], wholes[1], kv_wholes[0], kv_wholes[1])


def solution(mesh):
    placed = P(("group", "seq"), None)
    return jax.shard_map(
        on_device,
        mesh=mesh,
        in_specs=(placed, placed, placed, placed, P("group")),
        out_specs=(placed, placed, placed, placed),
        check_vma=False,
    )
```

```python
import functools
import math

import jax
import jax.numpy as jnp
from jax import lax
from jax.experimental import pallas as pl
from jax.experimental.pallas import tpu as pltpu
from jax.sharding import PartitionSpec as P

H = 32
KV = 8
HD = 128
MOST = 1024
GROUP = H // KV
KR = 16
F32 = jnp.float32
BF16 = jnp.bfloat16
SCALE = 1.0 / math.sqrt(HD)
EXP2_SCALE = SCALE * math.log2(math.e)


def query_rows(lanes):
    return max(16, 128 // lanes)


def attend_kernel(head, lanes, depth, start_ref, begin_ref, place_ref, key_place_ref, *refs):
    refs = list(refs)
    take = lambda count: [refs.pop(0) for _ in range(count)]
    query_refs, kv_refs = take(lanes), take(depth)
    out_refs, grad_refs = take(lanes), take(depth)
    key_turned, value_turned, key_sum, value_sum, score_ref, out_sum, query_sum = refs
    rows = query_refs[0].shape[1]
    turn_rows = query_rows(lanes)
    key_tiles, query_tiles = rows // KR, rows // turn_rows
    tile = depth * lanes * KR
    span = lanes * GROUP * turn_rows

    def keys_of(which, step):
        at = pl.ds(pl.multiple_of(step * KR, KR), KR)
        return jnp.concatenate(
            [ref[:, which, at, :].reshape(lanes * KR, HD) for ref in kv_refs], axis=0
        )

    def queries_of(which, step):
        at = pl.ds(pl.multiple_of(step * turn_rows, turn_rows), turn_rows)
        return jnp.concatenate(
            [
                ref[which, at, (head * GROUP + j) * HD : (head * GROUP + j + 1) * HD]
                for j in range(GROUP)
                for ref in query_refs
            ],
            axis=0,
        )

    def put_queries(which, step, value):
        at = pl.ds(pl.multiple_of(step * turn_rows, turn_rows), turn_rows)
        for j in range(GROUP):
            for lane, ref in enumerate(out_refs):
                low = (j * lanes + lane) * turn_rows
                ref[which, at, j * HD : (j + 1) * HD] = value[low : low + turn_rows]

    @pl.loop(0, key_tiles)
    def _(step):
        key_turned[step] = keys_of(0, step).T
        value_turned[step] = keys_of(1, step).T
        key_sum[step] = jnp.zeros((tile, HD), F32)
        value_sum[step] = jnp.zeros((tile, HD), F32)

    @pl.loop(0, query_tiles)
    def _(turn):
        query, grad = queries_of(0, turn), queries_of(1, turn)
        query_t, grad_t = query.T, grad.T
        first = start_ref[turn]
        last = (turn + 1) * (turn_rows // KR)
        begin, place = begin_ref[turn], place_ref[turn]

        def solve(count):
            tops = jnp.full((8, span), -1e30, F32)
            steps = [last - count + i for i in range(count)]
            key_place = jnp.concatenate([key_place_ref[...]] * (span // 128), axis=1)
            for i, step in enumerate(steps):
                base = step * tile
                value = jnp.dot(keys_of(0, step), query_t, preferred_element_type=F32)
                allowed = key_place >= begin - base
                if i >= count - turn_rows // KR:
                    allowed = allowed & (key_place <= place - base)
                value = jnp.where(allowed, value, -1e30)
                score_ref[i] = value
                tops = jnp.maximum(tops, value.reshape(tile // 8, 8, span).max(axis=0))
            top = jnp.max(tops, axis=0, keepdims=True) * EXP2_SCALE
            total = jnp.zeros((8, span), F32)
            out_t = jnp.zeros((HD, span), F32)
            for i, step in enumerate(steps):
                weight = jnp.exp2(score_ref[i] * EXP2_SCALE - top)
                score_ref[i] = weight
                out_t += jnp.dot(
                    value_turned[step], weight.astype(BF16), preferred_element_type=F32
                )
                total += weight.reshape(tile // 8, 8, span).sum(axis=0)
            inverse = 1.0 / jnp.sum(total, axis=0, keepdims=True)
            out_t = (out_t * inverse).astype(BF16).astype(F32)
            delta = jnp.sum(out_t * grad_t.astype(F32), axis=0, keepdims=True)
            put_queries(0, turn, out_t.T.astype(BF16))
            query_total = jnp.zeros((HD, span), F32)
            for i, step in enumerate(steps):
                prob = score_ref[i] * inverse
                value_sum[step] += jnp.dot(prob.astype(BF16), grad, preferred_element_type=F32)
                grad_prob = jnp.dot(keys_of(1, step), grad_t, preferred_element_type=F32)
                grad_score = (prob * (grad_prob - delta)).astype(BF16)
                key_sum[step] += jnp.dot(grad_score, query, preferred_element_type=F32)
                query_total += jnp.dot(
                    key_turned[step], grad_score, preferred_element_type=F32
                )
            put_queries(1, turn, (query_total * SCALE).T.astype(BF16))

        for count in range(1, score_ref.shape[0] + 1):

            @pl.when(last - first == count)
            def _():
                solve(count)

    @pl.loop(0, key_tiles)
    def _(step):
        at = pl.ds(pl.multiple_of(step * KR, KR), KR)
        for which, total, factor in ((0, key_sum, SCALE), (1, value_sum, 1.0)):
            for k, ref in enumerate(grad_refs):
                low = k * lanes * KR
                part = total[step, low : low + lanes * KR, :] * factor
                ref[:, which, at, :] = part.astype(ref.dtype).reshape(lanes, KR, HD)


def attend(head, query_parts, kv_parts, starts, begins, places, key_places):
    lanes, depth = len(query_parts), len(kv_parts)
    rows = query_parts[0].shape[1]
    turn_rows = query_rows(lanes)
    tile, span = depth * lanes * KR, lanes * GROUP * turn_rows
    key_tiles = rows // KR
    reach = turn_rows // KR + -(-(MOST - 1) // tile)
    vmem = pl.BlockSpec(memory_space=pltpu.VMEM)
    pairs = GROUP * rows * lanes * 640
    return pl.pallas_call(
        functools.partial(attend_kernel, head, lanes, depth),
        out_shape=[jax.ShapeDtypeStruct((2, rows, GROUP * HD), BF16)] * lanes
        + [
            jax.ShapeDtypeStruct(part.shape, F32 if k == 0 or (k == 2 and depth == 4) else BF16)
            for k, part in enumerate(kv_parts)
        ],
        in_specs=[pl.BlockSpec(memory_space=pltpu.SMEM)] + [vmem] * (3 + lanes + depth),
        out_specs=[vmem] * (lanes + depth),
        scratch_shapes=[
            pltpu.VMEM((key_tiles, HD, tile), BF16),
            pltpu.VMEM((key_tiles, HD, tile), BF16),
            pltpu.VMEM((key_tiles, tile, HD), F32),
            pltpu.VMEM((key_tiles, tile, HD), F32),
            pltpu.VMEM((min(reach, key_tiles), tile, span), F32),
            pltpu.VMEM((HD, span), F32),
            pltpu.VMEM((HD, span), F32),
        ],
        compiler_params=pltpu.CompilerParams(vmem_limit_bytes=(40 if depth == 4 else 62) << 20),
        cost_estimate=pl.CostEstimate(
            flops=10 * HD * pairs, bytes_accessed=8 << 20, transcendentals=pairs
        ),
    )(starts, begins, places, key_places, *query_parts, *kv_parts)


def moved(tensor, target):
    devices = lax.axis_size("seq")
    return lax.ppermute(tensor, "seq", [(i, target(i)) for i in range(devices)])


def swapped(tensor, mask):
    return moved(tensor, lambda i: i ^ mask)


def middle_swapped(tensor, lanes):
    return moved(tensor, lambda i: i if i // lanes in (0, 3) else i ^ (3 * lanes))


def after(tensor, *others):
    return lax.optimization_barrier((tensor, others))[0]


def plain_exchange(query_cuts, kv_owns, lanes, depth, run):
    heads = len(kv_owns)
    query_parts = [query_cuts[0]] + [swapped(query_cuts[mask], mask) for mask in range(1, lanes)]
    outs_back, totals = [], []
    for h in range(heads):
        own = kv_owns[h]
        outs, parts = run(
            h, query_parts, [own] + [swapped(own, k * lanes) for k in range(1, depth)]
        )
        outs_back.append([outs[0]] + [swapped(outs[mask], mask) for mask in range(1, lanes)])
        total = parts[0]
        for k in range(1, depth):
            total = total + swapped(parts[k].astype(BF16), k * lanes).astype(F32)
        totals.append(total.astype(BF16))
    return outs_back, totals


def ordered_exchange(query_cuts, kv_owns, lanes, inner, run):
    one, two, three = lanes, 2 * lanes, 3 * lanes
    query_x, query_d = swapped(query_cuts[2], 2), swapped(query_cuts[3], 3)
    a_two = swapped(kv_owns[0], two)
    a_one = swapped(kv_owns[0], one)
    a_three = middle_swapped(kv_owns[0], lanes)
    b_two = swapped(after(kv_owns[1], a_one), two)
    a_passed = swapped(a_two, one)
    b_three = swapped(after(kv_owns[1], a_three), three)
    b_one = swapped(after(kv_owns[1], query_x), one)
    query_c = swapped(after(query_cuts[1], query_d), 1)
    query_parts = [query_cuts[0], query_c, query_x, query_d]
    a_parts = [kv_owns[0], a_one, a_two, jnp.where(inner, a_three, a_passed)]
    outs_a, sum_a = run(0, query_parts, a_parts)
    a_passed = swapped(sum_a[3], one)
    a_middle = middle_swapped(sum_a[3], lanes)
    out_ax = swapped(after(outs_a[2], b_two), 2)
    out_ad = swapped(after(outs_a[3], b_one), 3)
    out_ac = swapped(after(outs_a[1], out_ax), 1)
    outs_b, sum_b = run(1, query_parts, [kv_owns[1], b_one, b_two, b_three])

    def joined_two(parts, passed):
        return (parts[2] + jnp.where(inner, passed.astype(F32), 0.0)).astype(BF16)

    def total(parts, first, second, middle):
        value = parts[0] + first.astype(F32) + second.astype(F32)
        return (value + jnp.where(inner, middle.astype(F32), 0.0)).astype(BF16)

    a_two = swapped(joined_two(sum_a, a_passed), two)
    b_passed = swapped(sum_b[3], one)
    a_one = swapped(after(sum_a[1], a_middle), one)
    b_middle = middle_swapped(after(sum_b[3], out_ax), lanes)
    b_two = swapped(joined_two(sum_b, b_passed), two)
    b_one = swapped(after(sum_b[1], a_one), one)
    out_bx = swapped(after(outs_b[2], out_ad), 2)
    out_bd = swapped(after(outs_b[3], a_two), 3)
    out_bc = swapped(after(outs_b[1], out_bx), 1)
    totals = [total(sum_a, a_one, a_two, a_middle), total(sum_b, b_one, b_two, b_middle)]
    outs_back = [[outs_a[0], out_ac, out_ax, out_ad], [outs_b[0], out_bc, out_bx, out_bd]]
    return outs_back, totals


def on_device(queries, key_vectors, value_vectors, grad_output, document_ids):
    devices = lax.axis_size("seq")
    position = lax.axis_index("seq")
    rows = queries.shape[0]
    lanes = min(KV, devices // 4)
    depth = devices // lanes
    lane = position % lanes
    above = position - lane
    level = position // lanes
    inner = (level > 0) & (level < depth - 1)
    heads = KV // lanes
    wide, narrow = H * HD // lanes, KV * HD // lanes

    def cut(tensor, mask, width):
        return lax.dynamic_slice_in_dim(tensor, (lane ^ mask) * width, width, 1)

    def kv_cut(mask):
        both = jnp.stack([cut(key_vectors, mask, narrow), cut(value_vectors, mask, narrow)])
        return jnp.stack([both[:, :, h * HD : (h + 1) * HD] for h in range(heads)])

    def query_cut(mask):
        return jnp.stack([cut(queries, mask, wide), cut(grad_output, mask, wide)])

    kv_lanes = [kv_cut(0)] + [swapped(kv_cut(mask), mask) for mask in range(1, lanes)]
    queries, grad_output = (after(tensor, kv_lanes[1]) for tensor in (queries, grad_output))
    query_cuts = [query_cut(mask) for mask in range(lanes)]
    kv_owns = [jnp.stack([part[h] for part in kv_lanes]) for h in range(heads)]

    ids = document_ids.reshape(rows, devices)
    lane_masks = jnp.arange(lanes, dtype=jnp.int32)
    mine = above + (lane ^ lane_masks)
    column = jnp.arange(devices, dtype=jnp.int32)
    own_ids = jnp.sum(
        jnp.where(column[None, None, :] == mine[:, None, None], ids[None], 0), axis=-1
    )
    begin = jnp.sum(
        (document_ids[None, None, :] < own_ids[:, :, None]).astype(jnp.int32), axis=-1
    )
    place = jnp.arange(rows, dtype=jnp.int32)[None, :] * devices + mine[:, None]

    turn_rows = query_rows(lanes)

    def tiled(values):
        parts = values.reshape(lanes, rows // turn_rows, turn_rows).transpose(1, 0, 2)
        parts = parts.reshape(rows // turn_rows, 1, lanes * turn_rows)
        return jnp.tile(parts, (1, 1, GROUP))

    begins, places = tiled(begin), tiled(place)
    starts = jnp.min(begins, axis=(1, 2)) // (KR * devices)
    chunk = (jnp.arange(depth, dtype=jnp.int32) * lanes) ^ above
    key_place = (
        jnp.arange(KR, dtype=jnp.int32)[None, None, :] * devices
        + chunk[:, None, None]
        + (lane ^ lane_masks)[None, :, None]
    ).reshape(depth * lanes * KR, 1)
    key_places = jnp.broadcast_to(key_place, (depth * lanes * KR, 128))

    def run(h, query_parts, kv_parts):
        results = attend(h, query_parts, kv_parts, starts, begins, places, key_places)
        return results[:lanes], results[lanes:]

    if depth == 4 and lanes == 4 and heads == 2:
        outs_back, totals = ordered_exchange(query_cuts, kv_owns, lanes, inner, run)
    else:
        outs_back, totals = plain_exchange(query_cuts, kv_owns, lanes, depth, run)
    wholes = [jnp.zeros((rows, H * HD), BF16) for _ in range(2)]
    kv_wholes = [jnp.zeros((rows, KV * HD), BF16) for _ in range(2)]
    for h in range(heads):
        total = totals[h]
        kv_back = [total[0]] + [swapped(total[mask], mask) for mask in range(1, lanes)]
        for which in range(2):
            for mask in range(lanes):
                owner = lane ^ mask
                wholes[which] = lax.dynamic_update_slice_in_dim(
                    wholes[which], outs_back[h][mask][which], owner * wide + h * GROUP * HD, 1
                )
                kv_wholes[which] = lax.dynamic_update_slice_in_dim(
                    kv_wholes[which], kv_back[mask][which], owner * narrow + h * HD, 1
                )
    return (wholes[0], wholes[1], kv_wholes[0], kv_wholes[1])


def solution(mesh):
    placed = P(("group", "seq"), None)
    return jax.shard_map(
        on_device,
        mesh=mesh,
        in_specs=(placed, placed, placed, placed, P("group")),
        out_specs=(placed, placed, placed, placed),
        check_vma=False,
    )
```

```python
import functools
import math

import jax
import jax.numpy as jnp
from jax import lax
from jax.experimental import pallas as pl
from jax.experimental.pallas import tpu as pltpu
from jax.sharding import PartitionSpec as P

H = 32
KV = 8
HD = 128
MOST = 1024
GROUP = H // KV
KR = 16
F32 = jnp.float32
BF16 = jnp.bfloat16
SCALE = 1.0 / math.sqrt(HD)
EXP2_SCALE = SCALE * math.log2(math.e)


def query_rows(lanes):
    return max(16, 128 // lanes)


def attend_kernel(head, lanes, depth, start_ref, begin_ref, place_ref, key_place_ref, *refs):
    refs = list(refs)
    take = lambda count: [refs.pop(0) for _ in range(count)]
    query_refs, kv_refs = take(lanes), take(depth)
    out_refs, grad_refs = take(lanes), take(depth)
    key_turned, value_turned, key_sum, value_sum, score_ref, out_sum, query_sum = refs
    rows = query_refs[0].shape[1]
    turn_rows = query_rows(lanes)
    key_tiles, query_tiles = rows // KR, rows // turn_rows
    tile = depth * lanes * KR
    span = lanes * GROUP * turn_rows

    def keys_of(which, step):
        at = pl.ds(pl.multiple_of(step * KR, KR), KR)
        return jnp.concatenate(
            [ref[:, which, at, :].reshape(lanes * KR, HD) for ref in kv_refs], axis=0
        )

    def queries_of(which, step):
        at = pl.ds(pl.multiple_of(step * turn_rows, turn_rows), turn_rows)
        return jnp.concatenate(
            [
                ref[which, at, (head * GROUP + j) * HD : (head * GROUP + j + 1) * HD]
                for j in range(GROUP)
                for ref in query_refs
            ],
            axis=0,
        )

    def put_queries(which, step, value):
        at = pl.ds(pl.multiple_of(step * turn_rows, turn_rows), turn_rows)
        for j in range(GROUP):
            for lane, ref in enumerate(out_refs):
                low = (j * lanes + lane) * turn_rows
                ref[which, at, j * HD : (j + 1) * HD] = value[low : low + turn_rows]

    @pl.loop(0, key_tiles)
    def _(step):
        key_turned[step] = keys_of(0, step).T
        value_turned[step] = keys_of(1, step).T
        key_sum[step] = jnp.zeros((tile, HD), F32)
        value_sum[step] = jnp.zeros((tile, HD), F32)

    @pl.loop(0, query_tiles)
    def _(turn):
        query, grad = queries_of(0, turn), queries_of(1, turn)
        query_t, grad_t = query.T, grad.T
        first = start_ref[turn]
        last = (turn + 1) * (turn_rows // KR)
        begin, place = begin_ref[turn], place_ref[turn]

        def solve(count):
            tops = jnp.full((8, span), -1e30, F32)
            steps = [last - count + i for i in range(count)]
            key_place = jnp.concatenate([key_place_ref[...]] * (span // 128), axis=1)
            for i, step in enumerate(steps):
                base = step * tile
                value = jnp.dot(keys_of(0, step), query_t, preferred_element_type=F32)
                allowed = key_place >= begin - base
                if i >= count - turn_rows // KR:
                    allowed = allowed & (key_place <= place - base)
                value = jnp.where(allowed, value, -1e30)
                score_ref[i] = value
                tops = jnp.maximum(tops, value.reshape(tile // 8, 8, span).max(axis=0))
            top = jnp.max(tops, axis=0, keepdims=True) * EXP2_SCALE
            total = jnp.zeros((8, span), F32)
            out_t = jnp.zeros((HD, span), F32)
            for i, step in enumerate(steps):
                weight = jnp.exp2(score_ref[i] * EXP2_SCALE - top)
                score_ref[i] = weight
                out_t += jnp.dot(
                    value_turned[step], weight.astype(BF16), preferred_element_type=F32
                )
                total += weight.reshape(tile // 8, 8, span).sum(axis=0)
            inverse = 1.0 / jnp.sum(total, axis=0, keepdims=True)
            out_t = (out_t * inverse).astype(BF16).astype(F32)
            delta = jnp.sum(out_t * grad_t.astype(F32), axis=0, keepdims=True)
            put_queries(0, turn, out_t.T.astype(BF16))
            query_total = jnp.zeros((HD, span), F32)
            for i, step in enumerate(steps):
                prob = score_ref[i] * inverse
                value_sum[step] += jnp.dot(prob.astype(BF16), grad, preferred_element_type=F32)
                grad_prob = jnp.dot(keys_of(1, step), grad_t, preferred_element_type=F32)
                grad_score = (prob * (grad_prob - delta)).astype(BF16)
                key_sum[step] += jnp.dot(grad_score, query, preferred_element_type=F32)
                query_total += jnp.dot(
                    key_turned[step], grad_score, preferred_element_type=F32
                )
            put_queries(1, turn, (query_total * SCALE).T.astype(BF16))

        for count in range(1, score_ref.shape[0] + 1):

            @pl.when(last - first == count)
            def _():
                solve(count)

    @pl.loop(0, key_tiles)
    def _(step):
        at = pl.ds(pl.multiple_of(step * KR, KR), KR)
        for which, total, factor in ((0, key_sum, SCALE), (1, value_sum, 1.0)):
            for k, ref in enumerate(grad_refs):
                low = k * lanes * KR
                part = total[step, low : low + lanes * KR, :] * factor
                ref[:, which, at, :] = part.astype(ref.dtype).reshape(lanes, KR, HD)


def attend(head, query_parts, kv_parts, starts, begins, places, key_places):
    lanes, depth = len(query_parts), len(kv_parts)
    rows = query_parts[0].shape[1]
    turn_rows = query_rows(lanes)
    tile, span = depth * lanes * KR, lanes * GROUP * turn_rows
    key_tiles = rows // KR
    reach = turn_rows // KR + -(-(MOST - 1) // tile)
    vmem = pl.BlockSpec(memory_space=pltpu.VMEM)
    pairs = GROUP * rows * lanes * 640
    return pl.pallas_call(
        functools.partial(attend_kernel, head, lanes, depth),
        out_shape=[jax.ShapeDtypeStruct((2, rows, GROUP * HD), BF16)] * lanes
        + [
            jax.ShapeDtypeStruct(part.shape, F32 if k == 0 or (k == 2 and depth == 4) else BF16)
            for k, part in enumerate(kv_parts)
        ],
        in_specs=[pl.BlockSpec(memory_space=pltpu.SMEM)] + [vmem] * (3 + lanes + depth),
        out_specs=[vmem] * (lanes + depth),
        scratch_shapes=[
            pltpu.VMEM((key_tiles, HD, tile), BF16),
            pltpu.VMEM((key_tiles, HD, tile), BF16),
            pltpu.VMEM((key_tiles, tile, HD), F32),
            pltpu.VMEM((key_tiles, tile, HD), F32),
            pltpu.VMEM((min(reach, key_tiles), tile, span), F32),
            pltpu.VMEM((HD, span), F32),
            pltpu.VMEM((HD, span), F32),
        ],
        compiler_params=pltpu.CompilerParams(vmem_limit_bytes=(40 if depth == 4 else 62) << 20),
        cost_estimate=pl.CostEstimate(
            flops=80 * HD * pairs, bytes_accessed=8 << 20, transcendentals=pairs
        ),
    )(starts, begins, places, key_places, *query_parts, *kv_parts)


def moved(tensor, target):
    devices = lax.axis_size("seq")
    return lax.ppermute(tensor, "seq", [(i, target(i)) for i in range(devices)])


def swapped(tensor, mask):
    return moved(tensor, lambda i: i ^ mask)


def middle_swapped(tensor, lanes):
    return moved(tensor, lambda i: i if i // lanes in (0, 3) else i ^ (3 * lanes))


def after(tensor, *others):
    return lax.optimization_barrier((tensor, others))[0]


def plain_exchange(query_cuts, kv_owns, lanes, depth, run):
    heads = len(kv_owns)
    query_parts = [query_cuts[0]] + [swapped(query_cuts[mask], mask) for mask in range(1, lanes)]
    outs_back, totals = [], []
    for h in range(heads):
        own = kv_owns[h]
        outs, parts = run(
            h, query_parts, [own] + [swapped(own, k * lanes) for k in range(1, depth)]
        )
        outs_back.append([outs[0]] + [swapped(outs[mask], mask) for mask in range(1, lanes)])
        total = parts[0]
        for k in range(1, depth):
            total = total + swapped(parts[k].astype(BF16), k * lanes).astype(F32)
        totals.append(total.astype(BF16))
    return outs_back, totals


def ordered_exchange(query_cuts, kv_owns, lanes, inner, run):
    one, two, three = lanes, 2 * lanes, 3 * lanes
    query_x, query_d = swapped(query_cuts[2], 2), swapped(query_cuts[3], 3)
    a_two = swapped(kv_owns[0], two)
    a_one = swapped(kv_owns[0], one)
    a_three = middle_swapped(kv_owns[0], lanes)
    b_two = swapped(after(kv_owns[1], a_one), two)
    a_passed = swapped(a_two, one)
    b_three = swapped(after(kv_owns[1], a_three), three)
    b_one = swapped(after(kv_owns[1], query_x), one)
    query_c = swapped(after(query_cuts[1], query_d), 1)
    query_parts = [query_cuts[0], query_c, query_x, query_d]
    a_parts = [kv_owns[0], a_one, a_two, jnp.where(inner, a_three, a_passed)]
    def joined_two(parts, passed):
        return (parts[2] + jnp.where(inner, passed.astype(F32), 0.0)).astype(BF16)

    def total(parts, first, second, middle):
        value = parts[0] + first.astype(F32) + second.astype(F32)
        return (value + jnp.where(inner, middle.astype(F32), 0.0)).astype(BF16)

    outs_a, sum_a = run(0, query_parts, a_parts)
    a_passed = swapped(sum_a[3], one)
    a_middle = middle_swapped(sum_a[3], lanes)
    a_two = swapped(joined_two(sum_a, a_passed), two)
    a_one = swapped(after(sum_a[1], b_one), one)
    out_ax = swapped(after(outs_a[2], b_two), 2)
    out_ad = swapped(after(outs_a[3], b_one), 3)
    outs_b, sum_b = run(
        1, query_parts, after([kv_owns[1], b_one, b_two, b_three], a_passed)
    )
    outs_b, sum_b = after((outs_b, sum_b), a_two, a_one, a_middle, out_ax, out_ad)
    b_passed = swapped(sum_b[3], one)
    out_ac = swapped(after(outs_a[1], a_one), 1)
    b_middle = middle_swapped(sum_b[3], lanes)
    out_bx = swapped(outs_b[2], 2)
    out_bd = swapped(outs_b[3], 3)
    b_send = joined_two(sum_b, b_passed)
    b_two = swapped(b_send, two)
    b_one = swapped(after(sum_b[1], b_send), one)
    out_bc = swapped(after(outs_b[1], out_bx), 1)
    totals = [
        after(total(sum_a, a_one, a_two, a_middle), out_bx),
        total(sum_b, b_one, b_two, b_middle),
    ]
    outs_back = [[outs_a[0], out_ac, out_ax, out_ad], [outs_b[0], out_bc, out_bx, out_bd]]
    return outs_back, totals


def on_device(queries, key_vectors, value_vectors, grad_output, document_ids):
    devices = lax.axis_size("seq")
    position = lax.axis_index("seq")
    rows = queries.shape[0]
    lanes = min(KV, devices // 4)
    depth = devices // lanes
    lane = position % lanes
    above = position - lane
    level = position // lanes
    inner = (level > 0) & (level < depth - 1)
    heads = KV // lanes
    wide, narrow = H * HD // lanes, KV * HD // lanes

    def cut(tensor, mask, width):
        return lax.dynamic_slice_in_dim(tensor, (lane ^ mask) * width, width, 1)

    def kv_cut(mask):
        both = jnp.stack([cut(key_vectors, mask, narrow), cut(value_vectors, mask, narrow)])
        return jnp.stack([both[:, :, h * HD : (h + 1) * HD] for h in range(heads)])

    def query_cut(mask):
        return jnp.stack([cut(queries, mask, wide), cut(grad_output, mask, wide)])

    kv_lanes = [kv_cut(0)] + [swapped(kv_cut(mask), mask) for mask in range(1, lanes)]
    queries, grad_output = (after(tensor, kv_lanes[1]) for tensor in (queries, grad_output))
    query_cuts = [query_cut(mask) for mask in range(lanes)]
    kv_owns = [jnp.stack([part[h] for part in kv_lanes]) for h in range(heads)]

    ids = document_ids.reshape(rows, devices)
    lane_masks = jnp.arange(lanes, dtype=jnp.int32)
    mine = above + (lane ^ lane_masks)
    column = jnp.arange(devices, dtype=jnp.int32)
    own_ids = jnp.sum(
        jnp.where(column[None, None, :] == mine[:, None, None], ids[None], 0), axis=-1
    )
    begin = jnp.sum(
        (document_ids[None, None, :] < own_ids[:, :, None]).astype(jnp.int32), axis=-1
    )
    place = jnp.arange(rows, dtype=jnp.int32)[None, :] * devices + mine[:, None]

    turn_rows = query_rows(lanes)

    def tiled(values):
        parts = values.reshape(lanes, rows // turn_rows, turn_rows).transpose(1, 0, 2)
        parts = parts.reshape(rows // turn_rows, 1, lanes * turn_rows)
        return jnp.tile(parts, (1, 1, GROUP))

    begins, places = tiled(begin), tiled(place)
    starts = jnp.min(begins, axis=(1, 2)) // (KR * devices)
    chunk = (jnp.arange(depth, dtype=jnp.int32) * lanes) ^ above
    key_place = (
        jnp.arange(KR, dtype=jnp.int32)[None, None, :] * devices
        + chunk[:, None, None]
        + (lane ^ lane_masks)[None, :, None]
    ).reshape(depth * lanes * KR, 1)
    key_places = jnp.broadcast_to(key_place, (depth * lanes * KR, 128))

    def run(h, query_parts, kv_parts):
        results = attend(h, query_parts, kv_parts, starts, begins, places, key_places)
        return results[:lanes], results[lanes:]

    if depth == 4 and lanes == 4 and heads == 2:
        outs_back, totals = ordered_exchange(query_cuts, kv_owns, lanes, inner, run)
    else:
        outs_back, totals = plain_exchange(query_cuts, kv_owns, lanes, depth, run)
    wholes = [jnp.zeros((rows, H * HD), BF16) for _ in range(2)]
    kv_wholes = [jnp.zeros((rows, KV * HD), BF16) for _ in range(2)]
    for h in range(heads):
        total = totals[h]
        kv_back = [total[0]] + [swapped(total[mask], mask) for mask in range(1, lanes)]
        for which in range(2):
            for mask in range(lanes):
                owner = lane ^ mask
                wholes[which] = lax.dynamic_update_slice_in_dim(
                    wholes[which], outs_back[h][mask][which], owner * wide + h * GROUP * HD, 1
                )
                kv_wholes[which] = lax.dynamic_update_slice_in_dim(
                    kv_wholes[which], kv_back[mask][which], owner * narrow + h * HD, 1
                )
    return (wholes[0], wholes[1], kv_wholes[0], kv_wholes[1])


def solution(mesh):
    placed = P(("group", "seq"), None)
    return jax.shard_map(
        on_device,
        mesh=mesh,
        in_specs=(placed, placed, placed, placed, P("group")),
        out_specs=(placed, placed, placed, placed),
        check_vma=False,
    )
```

```python
import functools
import math

import jax
import jax.numpy as jnp
from jax import lax
from jax.experimental import pallas as pl
from jax.experimental.pallas import tpu as pltpu
from jax.sharding import PartitionSpec as P

H = 32
KV = 8
HD = 128
MOST = 1024
GROUP = H // KV
KR = 16
F32 = jnp.float32
BF16 = jnp.bfloat16
SCALE = 1.0 / math.sqrt(HD)
EXP2_SCALE = SCALE * math.log2(math.e)


def query_rows(lanes):
    return max(16, 128 // lanes)


def attend_kernel(head, lanes, depth, start_ref, begin_ref, place_ref, key_place_ref, *refs):
    refs = list(refs)
    take = lambda count: [refs.pop(0) for _ in range(count)]
    query_refs, kv_refs = take(lanes), take(depth)
    out_refs, grad_refs = take(lanes), take(depth)
    key_turned, value_turned, key_sum, value_sum, score_ref, out_sum, query_sum = refs
    rows = query_refs[0].shape[1]
    turn_rows = query_rows(lanes)
    key_tiles, query_tiles = rows // KR, rows // turn_rows
    tile = depth * lanes * KR
    span = lanes * GROUP * turn_rows

    def keys_of(which, step):
        at = pl.ds(pl.multiple_of(step * KR, KR), KR)
        return jnp.concatenate(
            [ref[:, which, at, :].reshape(lanes * KR, HD) for ref in kv_refs], axis=0
        )

    def queries_of(which, step):
        at = pl.ds(pl.multiple_of(step * turn_rows, turn_rows), turn_rows)
        return jnp.concatenate(
            [
                ref[which, at, (head * GROUP + j) * HD : (head * GROUP + j + 1) * HD]
                for j in range(GROUP)
                for ref in query_refs
            ],
            axis=0,
        )

    def put_queries(which, step, value):
        at = pl.ds(pl.multiple_of(step * turn_rows, turn_rows), turn_rows)
        for j in range(GROUP):
            for lane, ref in enumerate(out_refs):
                low = (j * lanes + lane) * turn_rows
                ref[which, at, j * HD : (j + 1) * HD] = value[low : low + turn_rows]

    @pl.loop(0, key_tiles)
    def _(step):
        key_turned[step] = keys_of(0, step).T
        value_turned[step] = keys_of(1, step).T
        key_sum[step] = jnp.zeros((tile, HD), F32)
        value_sum[step] = jnp.zeros((tile, HD), F32)

    @pl.loop(0, query_tiles)
    def _(turn):
        query, grad = queries_of(0, turn), queries_of(1, turn)
        query_t, grad_t = query.T, grad.T
        first = start_ref[turn]
        last = (turn + 1) * (turn_rows // KR)
        begin, place = begin_ref[turn], place_ref[turn]

        def solve(count):
            tops = jnp.full((8, span), -1e30, F32)
            steps = [last - count + i for i in range(count)]
            key_place = jnp.concatenate([key_place_ref[...]] * (span // 128), axis=1)
            for i, step in enumerate(steps):
                base = step * tile
                value = jnp.dot(keys_of(0, step), query_t, preferred_element_type=F32)
                allowed = key_place >= begin - base
                if i >= count - turn_rows // KR:
                    allowed = allowed & (key_place <= place - base)
                value = jnp.where(allowed, value, -1e30)
                score_ref[i] = value
                tops = jnp.maximum(tops, value.reshape(tile // 8, 8, span).max(axis=0))
            top = jnp.max(tops, axis=0, keepdims=True) * EXP2_SCALE
            total = jnp.zeros((8, span), F32)
            out_t = jnp.zeros((HD, span), F32)
            for i, step in enumerate(steps):
                weight = jnp.exp2(score_ref[i] * EXP2_SCALE - top)
                score_ref[i] = weight
                out_t += jnp.dot(
                    value_turned[step], weight.astype(BF16), preferred_element_type=F32
                )
                total += weight.reshape(tile // 8, 8, span).sum(axis=0)
            inverse = 1.0 / jnp.sum(total, axis=0, keepdims=True)
            out_t = (out_t * inverse).astype(BF16).astype(F32)
            delta = jnp.sum(out_t * grad_t.astype(F32), axis=0, keepdims=True)
            put_queries(0, turn, out_t.T.astype(BF16))
            query_total = jnp.zeros((HD, span), F32)
            for i, step in enumerate(steps):
                prob = score_ref[i] * inverse
                value_sum[step] += jnp.dot(prob.astype(BF16), grad, preferred_element_type=F32)
                grad_prob = jnp.dot(keys_of(1, step), grad_t, preferred_element_type=F32)
                grad_score = (prob * (grad_prob - delta)).astype(BF16)
                key_sum[step] += jnp.dot(grad_score, query, preferred_element_type=F32)
                query_total += jnp.dot(
                    key_turned[step], grad_score, preferred_element_type=F32
                )
            put_queries(1, turn, (query_total * SCALE).T.astype(BF16))

        for count in range(1, score_ref.shape[0] + 1):

            @pl.when(last - first == count)
            def _():
                solve(count)

    @pl.loop(0, key_tiles)
    def _(step):
        at = pl.ds(pl.multiple_of(step * KR, KR), KR)
        for which, total, factor in ((0, key_sum, SCALE), (1, value_sum, 1.0)):
            for k, ref in enumerate(grad_refs):
                low = k * lanes * KR
                part = total[step, low : low + lanes * KR, :] * factor
                ref[:, which, at, :] = part.astype(ref.dtype).reshape(lanes, KR, HD)


def attend(head, query_parts, kv_parts, starts, begins, places, key_places):
    lanes, depth = len(query_parts), len(kv_parts)
    rows = query_parts[0].shape[1]
    turn_rows = query_rows(lanes)
    tile, span = depth * lanes * KR, lanes * GROUP * turn_rows
    key_tiles = rows // KR
    reach = turn_rows // KR + -(-(MOST - 1) // tile)
    vmem = pl.BlockSpec(memory_space=pltpu.VMEM)
    pairs = GROUP * rows * lanes * 640
    return pl.pallas_call(
        functools.partial(attend_kernel, head, lanes, depth),
        out_shape=[jax.ShapeDtypeStruct((2, rows, GROUP * HD), BF16)] * lanes
        + [
            jax.ShapeDtypeStruct(part.shape, F32 if k == 0 or (k == 2 and depth == 4) else BF16)
            for k, part in enumerate(kv_parts)
        ],
        in_specs=[pl.BlockSpec(memory_space=pltpu.SMEM)] + [vmem] * (3 + lanes + depth),
        out_specs=[vmem] * (lanes + depth),
        scratch_shapes=[
            pltpu.VMEM((key_tiles, HD, tile), BF16),
            pltpu.VMEM((key_tiles, HD, tile), BF16),
            pltpu.VMEM((key_tiles, tile, HD), F32),
            pltpu.VMEM((key_tiles, tile, HD), F32),
            pltpu.VMEM((min(reach, key_tiles), tile, span), F32),
            pltpu.VMEM((HD, span), F32),
            pltpu.VMEM((HD, span), F32),
        ],
        compiler_params=pltpu.CompilerParams(vmem_limit_bytes=(40 if depth == 4 else 62) << 20),
        cost_estimate=pl.CostEstimate(
            flops=80 * HD * pairs, bytes_accessed=8 << 20, transcendentals=pairs
        ),
    )(starts, begins, places, key_places, *query_parts, *kv_parts)


def moved(tensor, target):
    devices = lax.axis_size("seq")
    return lax.ppermute(tensor, "seq", [(i, target(i)) for i in range(devices)])


def swapped(tensor, mask):
    return moved(tensor, lambda i: i ^ mask)


def middle_swapped(tensor, lanes):
    return moved(tensor, lambda i: i if i // lanes in (0, 3) else i ^ (3 * lanes))


def after(tensor, *others):
    return lax.optimization_barrier((tensor, others))[0]


def plain_exchange(query_cuts, kv_owns, lanes, depth, run):
    heads = len(kv_owns)
    query_parts = [query_cuts[0]] + [swapped(query_cuts[mask], mask) for mask in range(1, lanes)]
    outs_back, totals = [], []
    for h in range(heads):
        own = kv_owns[h]
        outs, parts = run(
            h, query_parts, [own] + [swapped(own, k * lanes) for k in range(1, depth)]
        )
        outs_back.append([outs[0]] + [swapped(outs[mask], mask) for mask in range(1, lanes)])
        total = parts[0]
        for k in range(1, depth):
            total = total + swapped(parts[k].astype(BF16), k * lanes).astype(F32)
        totals.append(total.astype(BF16))
    return outs_back, totals


def ordered_exchange(query_cuts, kv_owns, lanes, inner, run):
    one, two, three = lanes, 2 * lanes, 3 * lanes
    query_x, query_d = swapped(query_cuts[2], 2), swapped(query_cuts[3], 3)
    a_two = swapped(kv_owns[0], two)
    a_one = swapped(kv_owns[0], one)
    a_three = middle_swapped(kv_owns[0], lanes)
    b_two = swapped(after(kv_owns[1], a_one), two)
    a_passed = swapped(a_two, one)
    b_three = swapped(after(kv_owns[1], a_three), three)
    b_one = swapped(after(kv_owns[1], query_x), one)
    query_c = swapped(after(query_cuts[1], query_d), 1)
    query_parts = [query_cuts[0], query_c, query_x, query_d]
    a_parts = [kv_owns[0], a_one, a_two, jnp.where(inner, a_three, a_passed)]
    def joined_two(parts, passed):
        return (parts[2] + jnp.where(inner, passed.astype(F32), 0.0)).astype(BF16)

    def total(parts, first, second, middle):
        value = parts[0] + first.astype(F32) + second.astype(F32)
        return (value + jnp.where(inner, middle.astype(F32), 0.0)).astype(BF16)

    outs_a, sum_a = run(0, query_parts, a_parts)
    a_one = swapped(sum_a[1], one)
    out_ax = swapped(outs_a[2], 2)
    a_two = swapped(after(sum_a[2].astype(BF16), b_two), two)
    a_three = swapped(after(sum_a[3], b_three), three)
    out_ad = swapped(after(outs_a[3], b_one), 3)
    outs_b, sum_b = run(1, query_parts, [kv_owns[1], b_one, b_two, b_three])
    outs_b, sum_b = after((outs_b, sum_b), a_two, a_one, a_three, out_ax, out_ad)
    b_passed = swapped(sum_b[3], one)
    out_ac = swapped(after(outs_a[1], a_one), 1)
    b_middle = middle_swapped(sum_b[3], lanes)
    out_bx = swapped(outs_b[2], 2)
    out_bd = swapped(outs_b[3], 3)
    b_send = joined_two(sum_b, b_passed)
    b_two = swapped(b_send, two)
    b_one = swapped(after(sum_b[1], b_send), one)
    out_bc = swapped(after(outs_b[1], out_bx), 1)
    totals = [
        after(
            (
                sum_a[0] + a_one.astype(F32) + a_two.astype(F32) + a_three.astype(F32)
            ).astype(BF16),
            out_bx,
        ),
        total(sum_b, b_one, b_two, b_middle),
    ]
    outs_back = [[outs_a[0], out_ac, out_ax, out_ad], [outs_b[0], out_bc, out_bx, out_bd]]
    return outs_back, totals


def on_device(queries, key_vectors, value_vectors, grad_output, document_ids):
    devices = lax.axis_size("seq")
    position = lax.axis_index("seq")
    rows = queries.shape[0]
    lanes = min(KV, devices // 4)
    depth = devices // lanes
    lane = position % lanes
    above = position - lane
    level = position // lanes
    inner = (level > 0) & (level < depth - 1)
    heads = KV // lanes
    wide, narrow = H * HD // lanes, KV * HD // lanes

    def cut(tensor, mask, width):
        return lax.dynamic_slice_in_dim(tensor, (lane ^ mask) * width, width, 1)

    def kv_cut(mask):
        both = jnp.stack([cut(key_vectors, mask, narrow), cut(value_vectors, mask, narrow)])
        return jnp.stack([both[:, :, h * HD : (h + 1) * HD] for h in range(heads)])

    def query_cut(mask):
        return jnp.stack([cut(queries, mask, wide), cut(grad_output, mask, wide)])

    kv_lanes = [kv_cut(0)] + [swapped(kv_cut(mask), mask) for mask in range(1, lanes)]
    queries, grad_output = (after(tensor, kv_lanes[1]) for tensor in (queries, grad_output))
    query_cuts = [query_cut(mask) for mask in range(lanes)]
    kv_owns = [jnp.stack([part[h] for part in kv_lanes]) for h in range(heads)]

    ids = document_ids.reshape(rows, devices)
    lane_masks = jnp.arange(lanes, dtype=jnp.int32)
    mine = above + (lane ^ lane_masks)
    column = jnp.arange(devices, dtype=jnp.int32)
    own_ids = jnp.sum(
        jnp.where(column[None, None, :] == mine[:, None, None], ids[None], 0), axis=-1
    )
    begin = jnp.sum(
        (document_ids[None, None, :] < own_ids[:, :, None]).astype(jnp.int32), axis=-1
    )
    place = jnp.arange(rows, dtype=jnp.int32)[None, :] * devices + mine[:, None]

    turn_rows = query_rows(lanes)

    def tiled(values):
        parts = values.reshape(lanes, rows // turn_rows, turn_rows).transpose(1, 0, 2)
        parts = parts.reshape(rows // turn_rows, 1, lanes * turn_rows)
        return jnp.tile(parts, (1, 1, GROUP))

    begins, places = tiled(begin), tiled(place)
    starts = jnp.min(begins, axis=(1, 2)) // (KR * devices)
    chunk = (jnp.arange(depth, dtype=jnp.int32) * lanes) ^ above
    key_place = (
        jnp.arange(KR, dtype=jnp.int32)[None, None, :] * devices
        + chunk[:, None, None]
        + (lane ^ lane_masks)[None, :, None]
    ).reshape(depth * lanes * KR, 1)
    key_places = jnp.broadcast_to(key_place, (depth * lanes * KR, 128))

    def run(h, query_parts, kv_parts):
        results = attend(h, query_parts, kv_parts, starts, begins, places, key_places)
        return results[:lanes], results[lanes:]

    if depth == 4 and lanes == 4 and heads == 2:
        outs_back, totals = ordered_exchange(query_cuts, kv_owns, lanes, inner, run)
    else:
        outs_back, totals = plain_exchange(query_cuts, kv_owns, lanes, depth, run)
    wholes = [jnp.zeros((rows, H * HD), BF16) for _ in range(2)]
    kv_wholes = [jnp.zeros((rows, KV * HD), BF16) for _ in range(2)]
    for h in range(heads):
        total = totals[h]
        kv_back = [total[0]] + [swapped(total[mask], mask) for mask in range(1, lanes)]
        for which in range(2):
            for mask in range(lanes):
                owner = lane ^ mask
                wholes[which] = lax.dynamic_update_slice_in_dim(
                    wholes[which], outs_back[h][mask][which], owner * wide + h * GROUP * HD, 1
                )
                kv_wholes[which] = lax.dynamic_update_slice_in_dim(
                    kv_wholes[which], kv_back[mask][which], owner * narrow + h * HD, 1
                )
    return (wholes[0], wholes[1], kv_wholes[0], kv_wholes[1])


def solution(mesh):
    placed = P(("group", "seq"), None)
    return jax.shard_map(
        on_device,
        mesh=mesh,
        in_specs=(placed, placed, placed, placed, P("group")),
        out_specs=(placed, placed, placed, placed),
        check_vma=False,
    )
```

```python
import functools
import math

import jax
import jax.numpy as jnp
from jax import lax
from jax.experimental import pallas as pl
from jax.experimental.pallas import tpu as pltpu
from jax.sharding import PartitionSpec as P

H = 32
KV = 8
HD = 128
MOST = 1024
GROUP = H // KV
KR = 16
F32 = jnp.float32
BF16 = jnp.bfloat16
SCALE = 1.0 / math.sqrt(HD)
EXP2_SCALE = SCALE * math.log2(math.e)


def query_rows(lanes):
    return max(16, 128 // lanes)


def attend_kernel(head, lanes, depth, start_ref, begin_ref, place_ref, key_place_ref, *refs):
    refs = list(refs)
    take = lambda count: [refs.pop(0) for _ in range(count)]
    query_refs, kv_refs = take(lanes), take(depth)
    out_refs, grad_refs = take(lanes), take(depth)
    key_turned, value_turned, key_sum, value_sum, score_ref, out_sum, query_sum = refs
    rows = query_refs[0].shape[1]
    turn_rows = query_rows(lanes)
    key_tiles, query_tiles = rows // KR, rows // turn_rows
    tile = depth * lanes * KR
    span = lanes * GROUP * turn_rows

    def keys_of(which, step):
        at = pl.ds(pl.multiple_of(step * KR, KR), KR)
        return jnp.concatenate(
            [ref[:, which, at, :].reshape(lanes * KR, HD) for ref in kv_refs], axis=0
        )

    def queries_of(which, step):
        at = pl.ds(pl.multiple_of(step * turn_rows, turn_rows), turn_rows)
        return jnp.concatenate(
            [
                ref[which, at, (head * GROUP + j) * HD : (head * GROUP + j + 1) * HD]
                for j in range(GROUP)
                for ref in query_refs
            ],
            axis=0,
        )

    def put_queries(which, step, value):
        at = pl.ds(pl.multiple_of(step * turn_rows, turn_rows), turn_rows)
        for j in range(GROUP):
            for lane, ref in enumerate(out_refs):
                low = (j * lanes + lane) * turn_rows
                ref[which, at, j * HD : (j + 1) * HD] = value[low : low + turn_rows]

    @pl.loop(0, key_tiles)
    def _(step):
        key_turned[step] = keys_of(0, step).T
        value_turned[step] = keys_of(1, step).T
        key_sum[step] = jnp.zeros((tile, HD), F32)
        value_sum[step] = jnp.zeros((tile, HD), F32)

    @pl.loop(0, query_tiles)
    def _(turn):
        query, grad = queries_of(0, turn), queries_of(1, turn)
        query_t, grad_t = query.T, grad.T
        first = start_ref[turn]
        last = (turn + 1) * (turn_rows // KR)
        begin, place = begin_ref[turn], place_ref[turn]

        def solve(count):
            tops = jnp.full((8, span), -1e30, F32)
            steps = [last - count + i for i in range(count)]
            key_place = jnp.concatenate([key_place_ref[...]] * (span // 128), axis=1)
            for i, step in enumerate(steps):
                base = step * tile
                value = jnp.dot(keys_of(0, step), query_t, preferred_element_type=F32)
                allowed = key_place >= begin - base
                if i >= count - turn_rows // KR:
                    allowed = allowed & (key_place <= place - base)
                value = jnp.where(allowed, value, -1e30)
                score_ref[i] = value
                tops = jnp.maximum(tops, value.reshape(tile // 8, 8, span).max(axis=0))
            top = jnp.max(tops, axis=0, keepdims=True) * EXP2_SCALE
            total = jnp.zeros((8, span), F32)
            out_t = jnp.zeros((HD, span), F32)
            for i, step in enumerate(steps):
                weight = jnp.exp2(score_ref[i] * EXP2_SCALE - top)
                score_ref[i] = weight
                out_t += jnp.dot(
                    value_turned[step], weight.astype(BF16), preferred_element_type=F32
                )
                total += weight.reshape(tile // 8, 8, span).sum(axis=0)
            inverse = 1.0 / jnp.sum(total, axis=0, keepdims=True)
            out_t = (out_t * inverse).astype(BF16).astype(F32)
            delta = jnp.sum(out_t * grad_t.astype(F32), axis=0, keepdims=True)
            put_queries(0, turn, out_t.T.astype(BF16))
            query_total = jnp.zeros((HD, span), F32)
            for i, step in enumerate(steps):
                prob = score_ref[i] * inverse
                value_sum[step] += jnp.dot(prob.astype(BF16), grad, preferred_element_type=F32)
                grad_prob = jnp.dot(keys_of(1, step), grad_t, preferred_element_type=F32)
                grad_score = (prob * (grad_prob - delta)).astype(BF16)
                key_sum[step] += jnp.dot(grad_score, query, preferred_element_type=F32)
                query_total += jnp.dot(
                    key_turned[step], grad_score, preferred_element_type=F32
                )
            put_queries(1, turn, (query_total * SCALE).T.astype(BF16))

        for count in range(1, score_ref.shape[0] + 1):

            @pl.when(last - first == count)
            def _():
                solve(count)

    @pl.loop(0, key_tiles)
    def _(step):
        at = pl.ds(pl.multiple_of(step * KR, KR), KR)
        for which, total, factor in ((0, key_sum, SCALE), (1, value_sum, 1.0)):
            for k, ref in enumerate(grad_refs):
                low = k * lanes * KR
                part = total[step, low : low + lanes * KR, :] * factor
                ref[:, which, at, :] = part.astype(ref.dtype).reshape(lanes, KR, HD)


def attend(head, query_parts, kv_parts, starts, begins, places, key_places):
    lanes, depth = len(query_parts), len(kv_parts)
    rows = query_parts[0].shape[1]
    turn_rows = query_rows(lanes)
    tile, span = depth * lanes * KR, lanes * GROUP * turn_rows
    key_tiles = rows // KR
    reach = turn_rows // KR + -(-(MOST - 1) // tile)
    vmem = pl.BlockSpec(memory_space=pltpu.VMEM)
    pairs = GROUP * rows * lanes * 640
    return pl.pallas_call(
        functools.partial(attend_kernel, head, lanes, depth),
        out_shape=[jax.ShapeDtypeStruct((2, rows, GROUP * HD), BF16)] * lanes
        + [
            jax.ShapeDtypeStruct(part.shape, F32 if k == 0 or (k == 2 and depth == 4) else BF16)
            for k, part in enumerate(kv_parts)
        ],
        in_specs=[pl.BlockSpec(memory_space=pltpu.SMEM)] + [vmem] * (3 + lanes + depth),
        out_specs=[vmem] * (lanes + depth),
        scratch_shapes=[
            pltpu.VMEM((key_tiles, HD, tile), BF16),
            pltpu.VMEM((key_tiles, HD, tile), BF16),
            pltpu.VMEM((key_tiles, tile, HD), F32),
            pltpu.VMEM((key_tiles, tile, HD), F32),
            pltpu.VMEM((min(reach, key_tiles), tile, span), F32),
            pltpu.VMEM((HD, span), F32),
            pltpu.VMEM((HD, span), F32),
        ],
        compiler_params=pltpu.CompilerParams(vmem_limit_bytes=(40 if depth == 4 else 62) << 20),
        cost_estimate=pl.CostEstimate(
            flops=80 * HD * pairs, bytes_accessed=8 << 20, transcendentals=pairs
        ),
    )(starts, begins, places, key_places, *query_parts, *kv_parts)


def moved(tensor, target):
    devices = lax.axis_size("seq")
    return lax.ppermute(tensor, "seq", [(i, target(i)) for i in range(devices)])


def swapped(tensor, mask):
    return moved(tensor, lambda i: i ^ mask)


def middle_swapped(tensor, lanes):
    return moved(tensor, lambda i: i if i // lanes in (0, 3) else i ^ (3 * lanes))


def after(tensor, *others):
    return lax.optimization_barrier((tensor, others))[0]


def plain_exchange(query_cuts, kv_owns, lanes, depth, run):
    heads = len(kv_owns)
    query_parts = [query_cuts[0]] + [swapped(query_cuts[mask], mask) for mask in range(1, lanes)]
    outs_back, totals = [], []
    for h in range(heads):
        own = kv_owns[h]
        outs, parts = run(
            h, query_parts, [own] + [swapped(own, k * lanes) for k in range(1, depth)]
        )
        outs_back.append([outs[0]] + [swapped(outs[mask], mask) for mask in range(1, lanes)])
        total = parts[0]
        for k in range(1, depth):
            total = total + swapped(parts[k].astype(BF16), k * lanes).astype(F32)
        totals.append(total.astype(BF16))
    return outs_back, totals


def ordered_exchange(query_cuts, kv_owns, lanes, inner, run):
    one, two, three = lanes, 2 * lanes, 3 * lanes
    query_d = swapped(query_cuts[3], 3)
    query_x = swapped(query_cuts[2], 2)
    a_one = swapped(kv_owns[0], one)
    a_near = middle_swapped(kv_owns[0], lanes)
    a_far = middle_swapped(after(a_one, query_d), lanes)
    a_two = swapped(a_near, one)
    a_three = swapped(a_far, one)
    b_two = swapped(after(kv_owns[1], a_far), two)
    b_three = swapped(after(kv_owns[1], a_two), three)
    b_one = swapped(after(kv_owns[1], a_three), one)
    query_c = swapped(after(query_cuts[1], a_two), 1)
    query_parts = [query_cuts[0], query_c, query_x, query_d]
    a_parts = [
        kv_owns[0],
        a_one,
        jnp.where(inner, a_far, a_two),
        jnp.where(inner, a_near, a_three),
    ]

    def joined_two(parts, passed):
        return (parts[2] + jnp.where(inner, passed.astype(F32), 0.0)).astype(BF16)

    def total(parts, first, second, middle):
        value = parts[0] + first.astype(F32) + second.astype(F32)
        return (value + jnp.where(inner, middle.astype(F32), 0.0)).astype(BF16)

    outs_a, sum_a = after(run(0, query_parts, a_parts), b_two, b_three, b_one)
    a_passed = swapped(sum_a[3], one)
    a_middle = middle_swapped(sum_a[3], lanes)
    a_two = swapped(joined_two(sum_a, a_passed), two)
    a_one = swapped(sum_a[1], one)
    outs_b, sum_b = run(
        1, query_parts, after([kv_owns[1], b_one, b_two, b_three], a_passed)
    )
    out_ax, out_ad = swapped(outs_a[2], 2), swapped(outs_a[3], 3)
    outs_b, sum_b = after((outs_b, sum_b), a_two, a_one, a_middle, out_ax, out_ad)
    b_passed = swapped(sum_b[3], one)
    out_ac = swapped(after(outs_a[1], b_passed), 1)
    b_middle = middle_swapped(sum_b[3], lanes)
    out_bx, out_bd = swapped(outs_b[2], 2), swapped(outs_b[3], 3)
    b_send = joined_two(sum_b, b_passed)
    b_two = swapped(b_send, two)
    b_one = swapped(after(sum_b[1], b_send), one)
    out_bc = swapped(after(outs_b[1], out_bx), 1)
    totals = [
        after(total(sum_a, a_one, a_two, a_middle), out_bx),
        total(sum_b, b_one, b_two, b_middle),
    ]
    outs_back = [[outs_a[0], out_ac, out_ax, out_ad], [outs_b[0], out_bc, out_bx, out_bd]]
    return outs_back, totals


def on_device(queries, key_vectors, value_vectors, grad_output, document_ids):
    devices = lax.axis_size("seq")
    position = lax.axis_index("seq")
    rows = queries.shape[0]
    lanes = min(KV, devices // 4)
    depth = devices // lanes
    lane = position % lanes
    above = position - lane
    level = position // lanes
    inner = (level > 0) & (level < depth - 1)
    heads = KV // lanes
    wide, narrow = H * HD // lanes, KV * HD // lanes

    def cut(tensor, mask, width):
        return lax.dynamic_slice_in_dim(tensor, (lane ^ mask) * width, width, 1)

    def kv_cut(mask):
        both = jnp.stack([cut(key_vectors, mask, narrow), cut(value_vectors, mask, narrow)])
        return jnp.stack([both[:, :, h * HD : (h + 1) * HD] for h in range(heads)])

    def query_cut(mask):
        return jnp.stack([cut(queries, mask, wide), cut(grad_output, mask, wide)])

    kv_lanes = [kv_cut(0)] + [swapped(kv_cut(mask), mask) for mask in range(1, lanes)]
    queries, grad_output = (after(tensor, kv_lanes[1]) for tensor in (queries, grad_output))
    query_cuts = [query_cut(mask) for mask in range(lanes)]
    kv_owns = [jnp.stack([part[h] for part in kv_lanes]) for h in range(heads)]

    ids = document_ids.reshape(rows, devices)
    lane_masks = jnp.arange(lanes, dtype=jnp.int32)
    mine = above + (lane ^ lane_masks)
    column = jnp.arange(devices, dtype=jnp.int32)
    own_ids = jnp.sum(
        jnp.where(column[None, None, :] == mine[:, None, None], ids[None], 0), axis=-1
    )
    begin = jnp.sum(
        (document_ids[None, None, :] < own_ids[:, :, None]).astype(jnp.int32), axis=-1
    )
    place = jnp.arange(rows, dtype=jnp.int32)[None, :] * devices + mine[:, None]

    turn_rows = query_rows(lanes)

    def tiled(values):
        parts = values.reshape(lanes, rows // turn_rows, turn_rows).transpose(1, 0, 2)
        parts = parts.reshape(rows // turn_rows, 1, lanes * turn_rows)
        return jnp.tile(parts, (1, 1, GROUP))

    begins, places = tiled(begin), tiled(place)
    starts = jnp.min(begins, axis=(1, 2)) // (KR * devices)
    chunk = (jnp.arange(depth, dtype=jnp.int32) * lanes) ^ above
    key_place = (
        jnp.arange(KR, dtype=jnp.int32)[None, None, :] * devices
        + chunk[:, None, None]
        + (lane ^ lane_masks)[None, :, None]
    ).reshape(depth * lanes * KR, 1)
    key_places = jnp.broadcast_to(key_place, (depth * lanes * KR, 128))

    def run(h, query_parts, kv_parts):
        results = attend(h, query_parts, kv_parts, starts, begins, places, key_places)
        return results[:lanes], results[lanes:]

    if depth == 4 and lanes == 4 and heads == 2:
        outs_back, totals = ordered_exchange(query_cuts, kv_owns, lanes, inner, run)
    else:
        outs_back, totals = plain_exchange(query_cuts, kv_owns, lanes, depth, run)
    wholes = [jnp.zeros((rows, H * HD), BF16) for _ in range(2)]
    kv_wholes = [jnp.zeros((rows, KV * HD), BF16) for _ in range(2)]
    for h in range(heads):
        total = totals[h]
        kv_back = [total[0]] + [swapped(total[mask], mask) for mask in range(1, lanes)]
        for which in range(2):
            for mask in range(lanes):
                owner = lane ^ mask
                wholes[which] = lax.dynamic_update_slice_in_dim(
                    wholes[which], outs_back[h][mask][which], owner * wide + h * GROUP * HD, 1
                )
                kv_wholes[which] = lax.dynamic_update_slice_in_dim(
                    kv_wholes[which], kv_back[mask][which], owner * narrow + h * HD, 1
                )
    return (wholes[0], wholes[1], kv_wholes[0], kv_wholes[1])


def solution(mesh):
    placed = P(("group", "seq"), None)
    return jax.shard_map(
        on_device,
        mesh=mesh,
        in_specs=(placed, placed, placed, placed, P("group")),
        out_specs=(placed, placed, placed, placed),
        check_vma=False,
    )
```

```python
import functools
import math

import jax
import jax.numpy as jnp
from jax import lax
from jax.experimental import pallas as pl
from jax.experimental.pallas import tpu as pltpu
from jax.sharding import PartitionSpec as P

H = 32
KV = 8
HD = 128
MOST = 1024
GROUP = H // KV
KR = 16
F32 = jnp.float32
BF16 = jnp.bfloat16
SCALE = 1.0 / math.sqrt(HD)
EXP2_SCALE = SCALE * math.log2(math.e)


def query_rows(lanes):
    return max(16, 128 // lanes)


def attend_kernel(lanes, depth, start_ref, begin_ref, *refs):
    refs = list(refs)
    take = lambda count: [refs.pop(0) for _ in range(count)]
    query_refs, kv_refs = take(lanes), take(depth)
    out_refs, grad_refs = take(lanes), take(depth)
    key_turned, value_turned, key_sum, value_sum, score_ref, key_place_ref = refs
    rows = query_refs[0].shape[1]
    turn_rows = query_rows(lanes)
    key_tiles, query_tiles = rows // KR, rows // turn_rows
    tile = depth * lanes * KR
    span = lanes * GROUP * turn_rows
    devices = lanes * depth
    position = lax.axis_index("seq")
    lane = lax.rem(position, lanes)
    above = position - lane
    at = lax.broadcasted_iota(jnp.int32, (tile, 128), 0)
    key_place_ref[...] = (
        lax.rem(at, KR) * devices
        + ((at // (KR * lanes) * lanes) ^ above)
        + (lax.rem(at // KR, lanes) ^ lane)
    )
    at = lax.broadcasted_iota(jnp.int32, (1, lanes * turn_rows), 1)
    row_place = lax.rem(at, turn_rows) * devices + above + ((at // turn_rows) ^ lane)

    def widened(row):
        return jnp.concatenate([row] * GROUP, axis=1)

    def keys_of(which, step):
        at = pl.ds(pl.multiple_of(step * KR, KR), KR)
        return jnp.concatenate(
            [ref[:, which, at, :].reshape(lanes * KR, HD) for ref in kv_refs], axis=0
        )

    def queries_of(which, step):
        at = pl.ds(pl.multiple_of(step * turn_rows, turn_rows), turn_rows)
        return jnp.concatenate(
            [
                ref[which, at, j * HD : (j + 1) * HD]
                for j in range(GROUP)
                for ref in query_refs
            ],
            axis=0,
        )

    def put_queries(which, step, value):
        at = pl.ds(pl.multiple_of(step * turn_rows, turn_rows), turn_rows)
        for j in range(GROUP):
            for lane, ref in enumerate(out_refs):
                low = (j * lanes + lane) * turn_rows
                ref[which, at, j * HD : (j + 1) * HD] = value[low : low + turn_rows]

    @pl.loop(0, key_tiles)
    def _(step):
        key_turned[step] = keys_of(0, step).T
        value_turned[step] = keys_of(1, step).T
        key_sum[step] = jnp.zeros((tile, HD), F32)
        value_sum[step] = jnp.zeros((tile, HD), F32)

    @pl.loop(0, query_tiles)
    def _(turn):
        query, grad = queries_of(0, turn), queries_of(1, turn)
        query_t, grad_t = query.T, grad.T
        first = start_ref[turn]
        last = (turn + 1) * (turn_rows // KR)
        begin = widened(begin_ref[turn])
        place = widened(row_place + turn * (turn_rows * devices))

        def solve(count):
            tops = jnp.full((8, span), -1e30, F32)
            steps = [last - count + i for i in range(count)]
            key_place = jnp.concatenate([key_place_ref[...]] * (span // 128), axis=1)
            for i, step in enumerate(steps):
                base = step * tile
                value = jnp.dot(keys_of(0, step), query_t, preferred_element_type=F32)
                allowed = key_place >= begin - base
                if i >= count - turn_rows // KR:
                    allowed = allowed & (key_place <= place - base)
                value = jnp.where(allowed, value, -1e30)
                score_ref[i] = value
                tops = jnp.maximum(tops, value.reshape(tile // 8, 8, span).max(axis=0))
            top = jnp.max(tops, axis=0, keepdims=True) * EXP2_SCALE
            total = jnp.zeros((8, span), F32)
            out_t = jnp.zeros((HD, span), F32)
            for i, step in enumerate(steps):
                weight = jnp.exp2(score_ref[i] * EXP2_SCALE - top)
                score_ref[i] = weight
                out_t += jnp.dot(
                    value_turned[step], weight.astype(BF16), preferred_element_type=F32
                )
                total += weight.reshape(tile // 8, 8, span).sum(axis=0)
            inverse = 1.0 / jnp.sum(total, axis=0, keepdims=True)
            out_t = (out_t * inverse).astype(BF16).astype(F32)
            delta = jnp.sum(out_t * grad_t.astype(F32), axis=0, keepdims=True)
            put_queries(0, turn, out_t.T.astype(BF16))
            query_total = jnp.zeros((HD, span), F32)
            for i, step in enumerate(steps):
                prob = score_ref[i] * inverse
                value_sum[step] += jnp.dot(prob.astype(BF16), grad, preferred_element_type=F32)
                grad_prob = jnp.dot(keys_of(1, step), grad_t, preferred_element_type=F32)
                grad_score = (prob * (grad_prob - delta)).astype(BF16)
                key_sum[step] += jnp.dot(grad_score, query, preferred_element_type=F32)
                query_total += jnp.dot(
                    key_turned[step], grad_score, preferred_element_type=F32
                )
            put_queries(1, turn, (query_total * SCALE).T.astype(BF16))

        for count in range(1, score_ref.shape[0] + 1):

            @pl.when(last - first == count)
            def _():
                solve(count)

    @pl.loop(0, key_tiles)
    def _(step):
        at = pl.ds(pl.multiple_of(step * KR, KR), KR)
        for which, total, factor in ((0, key_sum, SCALE), (1, value_sum, 1.0)):
            for k, ref in enumerate(grad_refs):
                low = k * lanes * KR
                part = total[step, low : low + lanes * KR, :] * factor
                ref[:, which, at, :] = part.astype(ref.dtype).reshape(lanes, KR, HD)


def attend(query_parts, kv_parts, starts, begins):
    lanes, depth = len(query_parts), len(kv_parts)
    rows = query_parts[0].shape[1]
    turn_rows = query_rows(lanes)
    tile, span = depth * lanes * KR, lanes * GROUP * turn_rows
    key_tiles = rows // KR
    reach = turn_rows // KR + -(-(MOST - 1) // tile)
    vmem = pl.BlockSpec(memory_space=pltpu.VMEM)
    pairs = GROUP * rows * lanes * 640
    return pl.pallas_call(
        functools.partial(attend_kernel, lanes, depth),
        out_shape=[jax.ShapeDtypeStruct((2, rows, GROUP * HD), BF16)] * lanes
        + [
            jax.ShapeDtypeStruct(part.shape, F32 if k == 0 or (k == 2 and depth == 4) else BF16)
            for k, part in enumerate(kv_parts)
        ],
        in_specs=[pl.BlockSpec(memory_space=pltpu.SMEM)] + [vmem] * (1 + lanes + depth),
        out_specs=[vmem] * (lanes + depth),
        scratch_shapes=[
            pltpu.VMEM((key_tiles, HD, tile), BF16),
            pltpu.VMEM((key_tiles, HD, tile), BF16),
            pltpu.VMEM((key_tiles, tile, HD), F32),
            pltpu.VMEM((key_tiles, tile, HD), F32),
            pltpu.VMEM((min(reach, key_tiles), tile, span), F32),
            pltpu.VMEM((tile, 128), jnp.int32),
        ],
        compiler_params=pltpu.CompilerParams(vmem_limit_bytes=(40 if depth == 4 else 62) << 20),
        cost_estimate=pl.CostEstimate(
            flops=80 * HD * pairs, bytes_accessed=8 << 20, transcendentals=pairs
        ),
    )(starts, begins, *query_parts, *kv_parts)


def packed_by_lane(pair, lanes, pieces):
    rows, columns = pair[0].shape
    width = columns // lanes
    shape = (2, rows, width // pieces)

    def pack(*refs):
        lane = lax.rem(lax.axis_index("seq"), lanes)
        for which in range(2):
            for mask in range(lanes):
                for piece in range(pieces):
                    at = (lane ^ mask) * width + piece * (width // pieces)
                    columns = pl.ds(pl.multiple_of(at, 128), width // pieces)
                    refs[2 + piece * lanes + mask][which] = refs[which][:, columns]

    vmem = pl.BlockSpec(memory_space=pltpu.VMEM)
    return pl.pallas_call(
        pack,
        out_shape=[jax.ShapeDtypeStruct(shape, BF16)] * (lanes * pieces),
        in_specs=[vmem] * 2,
        out_specs=[vmem] * (lanes * pieces),
    )(*pair)


def stacked_by_piece(parts):
    _, rows, width = parts[0].shape
    pieces, lanes, width = width // HD, len(parts), HD

    def stack(*refs):
        for piece in range(pieces):
            for lane in range(lanes):
                refs[lanes + piece][lane] = refs[lane][:, :, piece * HD : (piece + 1) * HD]

    vmem = pl.BlockSpec(memory_space=pltpu.VMEM)
    return pl.pallas_call(
        stack,
        out_shape=[jax.ShapeDtypeStruct((lanes, 2, rows, width), BF16)] * pieces,
        in_specs=[vmem] * lanes,
        out_specs=[vmem] * pieces,
    )(*parts)


def moved(tensor, target):
    devices = lax.axis_size("seq")
    return lax.ppermute(tensor, "seq", [(i, target(i)) for i in range(devices)])


def swapped(tensor, mask):
    return moved(tensor, lambda i: i ^ mask)


def middle_swapped(tensor, lanes):
    return moved(tensor, lambda i: i if i // lanes in (0, 3) else i ^ (3 * lanes))


def after(tensor, *others):
    return lax.optimization_barrier((tensor, others))[0]


def plain_exchange(query_cuts, kv_owns, lanes, depth, run):
    heads = len(kv_owns)
    outs_back, totals = [], []
    for h in range(heads):
        own, cuts = kv_owns[h], query_cuts[h]
        outs, parts = run(
            [cuts[0]] + [swapped(cuts[mask], mask) for mask in range(1, lanes)],
            [own] + [swapped(own, k * lanes) for k in range(1, depth)],
        )
        outs_back.append([outs[0]] + [swapped(outs[mask], mask) for mask in range(1, lanes)])
        total = parts[0]
        for k in range(1, depth):
            total = total + swapped(parts[k].astype(BF16), k * lanes).astype(F32)
        totals.append(total.astype(BF16))
    return outs_back, totals


def ordered_exchange(query_cuts, kv_owns, lanes, inner, run):
    one, two, three = lanes, 2 * lanes, 3 * lanes
    cuts_a, cuts_b = query_cuts
    qa_x, qa_d, qa_c = (swapped(cuts_a[mask], mask) for mask in (2, 3, 1))
    a_one = swapped(kv_owns[0], one)
    a_near = middle_swapped(kv_owns[0], lanes)
    a_far = middle_swapped(a_one, lanes)
    a_two = swapped(a_near, one)
    a_three = swapped(after(a_far, qa_x, qa_d), one)
    b_two = swapped(after(kv_owns[1], a_far), two)
    b_three = swapped(after(kv_owns[1], a_two), three)
    b_one = swapped(after(kv_owns[1], a_three), one)
    qb_x = swapped(after(cuts_b[2], a_three), 2)
    qb_d = swapped(after(cuts_b[3], a_three), 3)
    qb_c = swapped(after(cuts_b[1], b_two), 1)
    a_parts = [
        kv_owns[0],
        a_one,
        jnp.where(inner, a_far, a_two),
        jnp.where(inner, a_near, a_three),
    ]

    def joined_two(parts, passed):
        return (parts[2] + jnp.where(inner, passed.astype(F32), 0.0)).astype(BF16)

    def total(parts, first, second, middle):
        value = parts[0] + first.astype(F32) + second.astype(F32)
        return (value + jnp.where(inner, middle.astype(F32), 0.0)).astype(BF16)

    outs_a, sum_a = after(
        run([cuts_a[0], qa_c, qa_x, qa_d], a_parts), b_two, b_three, b_one, qb_x, qb_d
    )
    a_passed = swapped(sum_a[3], one)
    a_middle = middle_swapped(sum_a[3], lanes)
    a_two = swapped(joined_two(sum_a, a_passed), two)
    a_one = swapped(sum_a[1], one)
    outs_b, sum_b = run([cuts_b[0], qb_c, qb_x, qb_d], [kv_owns[1], b_one, b_two, b_three])
    out_ax, out_ad = swapped(outs_a[2], 2), swapped(outs_a[3], 3)
    outs_b, sum_b = after((outs_b, sum_b), a_passed, a_one, a_middle, out_ax, out_ad)
    b_passed = swapped(sum_b[3], one)
    out_ac = swapped(after(outs_a[1], b_passed), 1)
    b_middle = middle_swapped(sum_b[3], lanes)
    out_bx, out_bd = swapped(outs_b[2], 2), swapped(outs_b[3], 3)
    b_send = joined_two(sum_b, b_passed)
    b_two = swapped(b_send, two)
    b_one = swapped(after(sum_b[1], b_send), one)
    out_bc = swapped(after(outs_b[1], out_bx), 1)
    totals = [
        after(total(sum_a, a_one, a_two, a_middle), out_bx),
        total(sum_b, b_one, b_two, b_middle),
    ]
    outs_back = [[outs_a[0], out_ac, out_ax, out_ad], [outs_b[0], out_bc, out_bx, out_bd]]
    return outs_back, totals


def on_device(queries, key_vectors, value_vectors, grad_output, document_ids):
    devices = lax.axis_size("seq")
    position = lax.axis_index("seq")
    rows = queries.shape[0]
    lanes = min(KV, devices // 4)
    depth = devices // lanes
    lane = position % lanes
    above = position - lane
    level = position // lanes
    inner = (level > 0) & (level < depth - 1)
    heads = KV // lanes
    wide, narrow = H * HD // lanes, KV * HD // lanes

    kv_cuts = packed_by_lane((key_vectors, value_vectors), lanes, 1)
    kv_lanes = [kv_cuts[0]] + [swapped(kv_cuts[mask], mask) for mask in range(1, lanes)]
    kv_owns = stacked_by_piece(kv_lanes)
    queries, grad_output = (after(tensor, kv_owns[0]) for tensor in (queries, grad_output))
    packs = packed_by_lane((queries, grad_output), lanes, heads)
    query_cuts = [packs[h * lanes : (h + 1) * lanes] for h in range(heads)]

    ids = document_ids.reshape(rows, devices)
    lane_masks = jnp.arange(lanes, dtype=jnp.int32)
    mine = above + (lane ^ lane_masks)
    column = jnp.arange(devices, dtype=jnp.int32)
    own_ids = jnp.sum(
        jnp.where(column[None, None, :] == mine[:, None, None], ids[None], 0), axis=-1
    )
    begin = jnp.sum(
        (document_ids[None, None, :] < own_ids[:, :, None]).astype(jnp.int32), axis=-1
    )

    turn_rows = query_rows(lanes)

    begins = begin.reshape(lanes, rows // turn_rows, turn_rows).transpose(1, 0, 2)
    starts = lax.div(jnp.min(begins, axis=(1, 2)), jnp.int32(KR * devices))
    begins = begins.reshape(rows // turn_rows, 1, lanes * turn_rows)

    def run(query_parts, kv_parts):
        results = attend(query_parts, kv_parts, starts, begins)
        return results[:lanes], results[lanes:]

    if depth == 4 and lanes == 4 and heads == 2:
        outs_back, totals = ordered_exchange(query_cuts, kv_owns, lanes, inner, run)
    else:
        outs_back, totals = plain_exchange(query_cuts, kv_owns, lanes, depth, run)
    wholes = [jnp.zeros((rows, H * HD), BF16) for _ in range(2)]
    kv_wholes = [jnp.zeros((rows, KV * HD), BF16) for _ in range(2)]
    for h in range(heads):
        total = totals[h]
        kv_back = [total[0]] + [swapped(total[mask], mask) for mask in range(1, lanes)]
        for which in range(2):
            for mask in range(lanes):
                owner = lane ^ mask
                wholes[which] = lax.dynamic_update_slice_in_dim(
                    wholes[which], outs_back[h][mask][which], owner * wide + h * GROUP * HD, 1
                )
                kv_wholes[which] = lax.dynamic_update_slice_in_dim(
                    kv_wholes[which], kv_back[mask][which], owner * narrow + h * HD, 1
                )
    return (wholes[0], wholes[1], kv_wholes[0], kv_wholes[1])


def solution(mesh):
    placed = P(("group", "seq"), None)
    return jax.shard_map(
        on_device,
        mesh=mesh,
        in_specs=(placed, placed, placed, placed, P("group")),
        out_specs=(placed, placed, placed, placed),
        check_vma=False,
    )
```

```python
import functools
import math

import jax
import jax.numpy as jnp
from jax import lax
from jax.experimental import pallas as pl
from jax.experimental.pallas import tpu as pltpu
from jax.sharding import PartitionSpec as P

H = 32
KV = 8
HD = 128
MOST = 1024
GROUP = H // KV
KR = 16
F32 = jnp.float32
BF16 = jnp.bfloat16
SCALE = 1.0 / math.sqrt(HD)
EXP2_SCALE = SCALE * math.log2(math.e)


def query_rows(lanes):
    return max(16, 128 // lanes)


def attend_kernel(head, lanes, depth, start_ref, begin_ref, place_ref, key_place_ref, *refs):
    refs = list(refs)
    take = lambda count: [refs.pop(0) for _ in range(count)]
    query_refs, kv_refs = take(lanes), take(depth)
    out_refs, grad_refs = take(lanes), take(depth)
    key_turned, value_turned, key_sum, value_sum, score_ref, out_sum, query_sum = refs
    rows = query_refs[0].shape[1]
    turn_rows = query_rows(lanes)
    key_tiles, query_tiles = rows // KR, rows // turn_rows
    tile = depth * lanes * KR
    span = lanes * GROUP * turn_rows

    def keys_of(which, step):
        at = pl.ds(pl.multiple_of(step * KR, KR), KR)
        return jnp.concatenate(
            [ref[:, which, at, :].reshape(lanes * KR, HD) for ref in kv_refs], axis=0
        )

    def queries_of(which, step):
        at = pl.ds(pl.multiple_of(step * turn_rows, turn_rows), turn_rows)
        return jnp.concatenate(
            [
                ref[which, at, (head * GROUP + j) * HD : (head * GROUP + j + 1) * HD]
                for j in range(GROUP)
                for ref in query_refs
            ],
            axis=0,
        )

    def put_queries(which, step, value):
        at = pl.ds(pl.multiple_of(step * turn_rows, turn_rows), turn_rows)
        for j in range(GROUP):
            for lane, ref in enumerate(out_refs):
                low = (j * lanes + lane) * turn_rows
                ref[which, at, j * HD : (j + 1) * HD] = value[low : low + turn_rows]

    @pl.loop(0, key_tiles)
    def _(step):
        key_turned[step] = keys_of(0, step).T
        value_turned[step] = keys_of(1, step).T
        key_sum[step] = jnp.zeros((tile, HD), F32)
        value_sum[step] = jnp.zeros((tile, HD), F32)

    @pl.loop(0, query_tiles)
    def _(turn):
        query, grad = queries_of(0, turn), queries_of(1, turn)
        query_t, grad_t = query.T, grad.T
        first = start_ref[turn]
        last = (turn + 1) * (turn_rows // KR)
        begin, place = begin_ref[turn], place_ref[turn]

        def solve(count):
            tops = jnp.full((8, span), -1e30, F32)
            steps = [last - count + i for i in range(count)]
            key_place = jnp.concatenate([key_place_ref[...]] * (span // 128), axis=1)
            for i, step in enumerate(steps):
                base = step * tile
                value = jnp.dot(keys_of(0, step), query_t, preferred_element_type=F32)
                allowed = key_place >= begin - base
                if i >= count - turn_rows // KR:
                    allowed = allowed & (key_place <= place - base)
                value = jnp.where(allowed, value, -1e30)
                score_ref[i] = value
                tops = jnp.maximum(tops, value.reshape(tile // 8, 8, span).max(axis=0))
            top = jnp.max(tops, axis=0, keepdims=True) * EXP2_SCALE
            total = jnp.zeros((8, span), F32)
            out_t = jnp.zeros((HD, span), F32)
            for i, step in enumerate(steps):
                weight = jnp.exp2(score_ref[i] * EXP2_SCALE - top)
                score_ref[i] = weight
                out_t += jnp.dot(
                    value_turned[step], weight.astype(BF16), preferred_element_type=F32
                )
                total += weight.reshape(tile // 8, 8, span).sum(axis=0)
            inverse = 1.0 / jnp.sum(total, axis=0, keepdims=True)
            out_t = (out_t * inverse).astype(BF16).astype(F32)
            delta = jnp.sum(out_t * grad_t.astype(F32), axis=0, keepdims=True)
            put_queries(0, turn, out_t.T.astype(BF16))
            query_total = jnp.zeros((HD, span), F32)
            for i, step in enumerate(steps):
                prob = score_ref[i] * inverse
                value_sum[step] += jnp.dot(prob.astype(BF16), grad, preferred_element_type=F32)
                grad_prob = jnp.dot(keys_of(1, step), grad_t, preferred_element_type=F32)
                grad_score = (prob * (grad_prob - delta)).astype(BF16)
                key_sum[step] += jnp.dot(grad_score, query, preferred_element_type=F32)
                query_total += jnp.dot(
                    key_turned[step], grad_score, preferred_element_type=F32
                )
            put_queries(1, turn, (query_total * SCALE).T.astype(BF16))

        for count in range(1, score_ref.shape[0] + 1):

            @pl.when(last - first == count)
            def _():
                solve(count)

    @pl.loop(0, key_tiles)
    def _(step):
        at = pl.ds(pl.multiple_of(step * KR, KR), KR)
        for which, total, factor in ((0, key_sum, SCALE), (1, value_sum, 1.0)):
            for k, ref in enumerate(grad_refs):
                low = k * lanes * KR
                part = total[step, low : low + lanes * KR, :] * factor
                ref[:, which, at, :] = part.astype(ref.dtype).reshape(lanes, KR, HD)


def attend(head, query_parts, kv_parts, starts, begins, places, key_places):
    lanes, depth = len(query_parts), len(kv_parts)
    rows = query_parts[0].shape[1]
    turn_rows = query_rows(lanes)
    tile, span = depth * lanes * KR, lanes * GROUP * turn_rows
    key_tiles = rows // KR
    reach = turn_rows // KR + -(-(MOST - 1) // tile)
    vmem = pl.BlockSpec(memory_space=pltpu.VMEM)
    pairs = GROUP * rows * lanes * 640
    return pl.pallas_call(
        functools.partial(attend_kernel, head, lanes, depth),
        out_shape=[jax.ShapeDtypeStruct((2, rows, GROUP * HD), BF16)] * lanes
        + [
            jax.ShapeDtypeStruct(part.shape, F32 if k == 0 or (k == 2 and depth == 4) else BF16)
            for k, part in enumerate(kv_parts)
        ],
        in_specs=[pl.BlockSpec(memory_space=pltpu.SMEM)] + [vmem] * (3 + lanes + depth),
        out_specs=[vmem] * (lanes + depth),
        scratch_shapes=[
            pltpu.VMEM((key_tiles, HD, tile), BF16),
            pltpu.VMEM((key_tiles, HD, tile), BF16),
            pltpu.VMEM((key_tiles, tile, HD), F32),
            pltpu.VMEM((key_tiles, tile, HD), F32),
            pltpu.VMEM((min(reach, key_tiles), tile, span), F32),
            pltpu.VMEM((HD, span), F32),
            pltpu.VMEM((HD, span), F32),
        ],
        compiler_params=pltpu.CompilerParams(vmem_limit_bytes=(40 if depth == 4 else 62) << 20),
        cost_estimate=pl.CostEstimate(
            flops=80 * HD * pairs, bytes_accessed=8 << 20, transcendentals=pairs
        ),
    )(starts, begins, places, key_places, *query_parts, *kv_parts)


def moved(tensor, target):
    devices = lax.axis_size("seq")
    return lax.ppermute(tensor, "seq", [(i, target(i)) for i in range(devices)])


def swapped(tensor, mask):
    return moved(tensor, lambda i: i ^ mask)


def middle_swapped(tensor, lanes):
    return moved(tensor, lambda i: i if i // lanes in (0, 3) else i ^ (3 * lanes))


def after(tensor, *others):
    return lax.optimization_barrier((tensor, others))[0]


def plain_exchange(query_cuts, kv_owns, lanes, depth, run):
    heads = len(kv_owns)
    query_parts = [query_cuts[0]] + [swapped(query_cuts[mask], mask) for mask in range(1, lanes)]
    outs_back, totals = [], []
    for h in range(heads):
        own = kv_owns[h]
        outs, parts = run(
            h, query_parts, [own] + [swapped(own, k * lanes) for k in range(1, depth)]
        )
        outs_back.append([outs[0]] + [swapped(outs[mask], mask) for mask in range(1, lanes)])
        total = parts[0]
        for k in range(1, depth):
            total = total + swapped(parts[k].astype(BF16), k * lanes).astype(F32)
        totals.append(total.astype(BF16))
    return outs_back, totals


def ordered_exchange(query_cuts, kv_owns, lanes, inner, run):
    one, two, three = lanes, 2 * lanes, 3 * lanes
    query_x, query_d = swapped(query_cuts[2], 2), swapped(query_cuts[3], 3)
    a_two = swapped(kv_owns[0], two)
    a_one = swapped(kv_owns[0], one)
    a_three = middle_swapped(kv_owns[0], lanes)
    a_passed = swapped(a_two, one)
    b_three = middle_swapped(after(kv_owns[1], a_three, a_one), lanes)
    b_two = swapped(after(kv_owns[1], a_passed), two)
    b_one = swapped(after(kv_owns[1], query_x), one)
    query_c = swapped(after(query_cuts[1], query_d), 1)
    query_parts = [query_cuts[0], query_c, query_x, query_d]
    a_parts = [kv_owns[0], a_one, a_two, jnp.where(inner, a_three, a_passed)]
    def joined_two(parts, passed):
        return (parts[2] + jnp.where(inner, passed.astype(F32), 0.0)).astype(BF16)

    def total(parts, first, second, middle):
        value = parts[0] + first.astype(F32) + second.astype(F32)
        return (value + jnp.where(inner, middle.astype(F32), 0.0)).astype(BF16)

    outs_a, sum_a = run(0, query_parts, a_parts)
    b_passed = swapped(after(b_two, sum_a[0]), one)
    b_three = jnp.where(inner, b_three, b_passed)
    a_passed = swapped(sum_a[3], one)
    a_middle = middle_swapped(sum_a[3], lanes)
    a_two = swapped(joined_two(sum_a, a_passed), two)
    a_one = swapped(after(sum_a[1], b_passed), one)
    out_ax = swapped(after(outs_a[2], b_one), 2)
    out_ad = swapped(after(outs_a[3], b_one), 3)
    outs_b, sum_b = run(
        1, query_parts, after([kv_owns[1], b_one, b_two, b_three], a_passed)
    )
    outs_b, sum_b = after((outs_b, sum_b), a_two, a_one, a_middle, out_ax, out_ad)
    b_passed = swapped(sum_b[3], one)
    out_ac = swapped(after(outs_a[1], a_one), 1)
    b_middle = middle_swapped(sum_b[3], lanes)
    out_bx = swapped(outs_b[2], 2)
    out_bd = swapped(outs_b[3], 3)
    b_send = joined_two(sum_b, b_passed)
    b_two = swapped(b_send, two)
    b_one = swapped(after(sum_b[1], b_send), one)
    out_bc = swapped(after(outs_b[1], out_bx), 1)
    totals = [
        after(total(sum_a, a_one, a_two, a_middle), out_bx),
        total(sum_b, b_one, b_two, b_middle),
    ]
    outs_back = [[outs_a[0], out_ac, out_ax, out_ad], [outs_b[0], out_bc, out_bx, out_bd]]
    return outs_back, totals


def on_device(queries, key_vectors, value_vectors, grad_output, document_ids):
    devices = lax.axis_size("seq")
    position = lax.axis_index("seq")
    rows = queries.shape[0]
    lanes = min(KV, devices // 4)
    depth = devices // lanes
    lane = position % lanes
    above = position - lane
    level = position // lanes
    inner = (level > 0) & (level < depth - 1)
    heads = KV // lanes
    wide, narrow = H * HD // lanes, KV * HD // lanes

    def cut(tensor, mask, width):
        return lax.dynamic_slice_in_dim(tensor, (lane ^ mask) * width, width, 1)

    def kv_cut(mask):
        both = jnp.stack([cut(key_vectors, mask, narrow), cut(value_vectors, mask, narrow)])
        return jnp.stack([both[:, :, h * HD : (h + 1) * HD] for h in range(heads)])

    def query_cut(mask):
        return jnp.stack([cut(queries, mask, wide), cut(grad_output, mask, wide)])

    kv_lanes = [kv_cut(0)] + [swapped(kv_cut(mask), mask) for mask in range(1, lanes)]
    queries, grad_output = (after(tensor, kv_lanes[1]) for tensor in (queries, grad_output))
    query_cuts = [query_cut(mask) for mask in range(lanes)]
    kv_owns = [jnp.stack([part[h] for part in kv_lanes]) for h in range(heads)]

    ids = document_ids.reshape(rows, devices)
    lane_masks = jnp.arange(lanes, dtype=jnp.int32)
    mine = above + (lane ^ lane_masks)
    column = jnp.arange(devices, dtype=jnp.int32)
    own_ids = jnp.sum(
        jnp.where(column[None, None, :] == mine[:, None, None], ids[None], 0), axis=-1
    )
    begin = jnp.sum(
        (document_ids[None, None, :] < own_ids[:, :, None]).astype(jnp.int32), axis=-1
    )
    place = jnp.arange(rows, dtype=jnp.int32)[None, :] * devices + mine[:, None]

    turn_rows = query_rows(lanes)

    def tiled(values):
        parts = values.reshape(lanes, rows // turn_rows, turn_rows).transpose(1, 0, 2)
        parts = parts.reshape(rows // turn_rows, 1, lanes * turn_rows)
        return jnp.tile(parts, (1, 1, GROUP))

    begins, places = tiled(begin), tiled(place)
    starts = jnp.min(begins, axis=(1, 2)) // (KR * devices)
    chunk = (jnp.arange(depth, dtype=jnp.int32) * lanes) ^ above
    key_place = (
        jnp.arange(KR, dtype=jnp.int32)[None, None, :] * devices
        + chunk[:, None, None]
        + (lane ^ lane_masks)[None, :, None]
    ).reshape(depth * lanes * KR, 1)
    key_places = jnp.broadcast_to(key_place, (depth * lanes * KR, 128))

    def run(h, query_parts, kv_parts):
        results = attend(h, query_parts, kv_parts, starts, begins, places, key_places)
        return results[:lanes], results[lanes:]

    if depth == 4 and lanes == 4 and heads == 2:
        outs_back, totals = ordered_exchange(query_cuts, kv_owns, lanes, inner, run)
    else:
        outs_back, totals = plain_exchange(query_cuts, kv_owns, lanes, depth, run)
    wholes = [jnp.zeros((rows, H * HD), BF16) for _ in range(2)]
    kv_wholes = [jnp.zeros((rows, KV * HD), BF16) for _ in range(2)]
    for h in range(heads):
        total = totals[h]
        kv_back = [total[0]] + [swapped(total[mask], mask) for mask in range(1, lanes)]
        for which in range(2):
            for mask in range(lanes):
                owner = lane ^ mask
                wholes[which] = lax.dynamic_update_slice_in_dim(
                    wholes[which], outs_back[h][mask][which], owner * wide + h * GROUP * HD, 1
                )
                kv_wholes[which] = lax.dynamic_update_slice_in_dim(
                    kv_wholes[which], kv_back[mask][which], owner * narrow + h * HD, 1
                )
    return (wholes[0], wholes[1], kv_wholes[0], kv_wholes[1])


def solution(mesh):
    placed = P(("group", "seq"), None)
    return jax.shard_map(
        on_device,
        mesh=mesh,
        in_specs=(placed, placed, placed, placed, P("group")),
        out_specs=(placed, placed, placed, placed),
        check_vma=False,
    )
```

```python
import functools
import math

import jax
import jax.numpy as jnp
from jax import lax
from jax.experimental import pallas as pl
from jax.experimental.pallas import tpu as pltpu
from jax.sharding import PartitionSpec as P

H = 32
KV = 8
HD = 128
MOST = 1024
GROUP = H // KV
KR = 16
F32 = jnp.float32
BF16 = jnp.bfloat16
SCALE = 1.0 / math.sqrt(HD)
EXP2_SCALE = SCALE * math.log2(math.e)


def query_rows(lanes):
    return max(16, 128 // lanes)


def attend_kernel(head, lanes, depth, start_ref, begin_ref, place_ref, key_place_ref, *refs):
    refs = list(refs)
    take = lambda count: [refs.pop(0) for _ in range(count)]
    query_refs, kv_refs = take(lanes), take(depth)
    out_refs, grad_refs = take(lanes), take(depth)
    key_turned, value_turned, key_sum, value_sum, score_ref, out_sum, query_sum = refs
    rows = query_refs[0].shape[1]
    turn_rows = query_rows(lanes)
    key_tiles, query_tiles = rows // KR, rows // turn_rows
    tile = depth * lanes * KR
    span = lanes * GROUP * turn_rows

    def keys_of(which, step):
        at = pl.ds(pl.multiple_of(step * KR, KR), KR)
        return jnp.concatenate(
            [ref[:, which, at, :].reshape(lanes * KR, HD) for ref in kv_refs], axis=0
        )

    def queries_of(which, step):
        at = pl.ds(pl.multiple_of(step * turn_rows, turn_rows), turn_rows)
        return jnp.concatenate(
            [
                ref[which, at, (head * GROUP + j) * HD : (head * GROUP + j + 1) * HD]
                for j in range(GROUP)
                for ref in query_refs
            ],
            axis=0,
        )

    def put_queries(which, step, value):
        at = pl.ds(pl.multiple_of(step * turn_rows, turn_rows), turn_rows)
        for j in range(GROUP):
            for lane, ref in enumerate(out_refs):
                low = (j * lanes + lane) * turn_rows
                ref[which, at, j * HD : (j + 1) * HD] = value[low : low + turn_rows]

    @pl.loop(0, key_tiles)
    def _(step):
        key_turned[step] = keys_of(0, step).T
        value_turned[step] = keys_of(1, step).T
        key_sum[step] = jnp.zeros((tile, HD), F32)
        value_sum[step] = jnp.zeros((tile, HD), F32)

    @pl.loop(0, query_tiles)
    def _(turn):
        query, grad = queries_of(0, turn), queries_of(1, turn)
        query_t, grad_t = query.T, grad.T
        first = start_ref[turn]
        last = (turn + 1) * (turn_rows // KR)
        begin, place = begin_ref[turn], place_ref[turn]

        def solve(count):
            tops = jnp.full((8, span), -1e30, F32)
            steps = [last - count + i for i in range(count)]
            key_place = jnp.concatenate([key_place_ref[...]] * (span // 128), axis=1)
            for i, step in enumerate(steps):
                base = step * tile
                value = jnp.dot(keys_of(0, step), query_t, preferred_element_type=F32)
                allowed = key_place >= begin - base
                if i >= count - turn_rows // KR:
                    allowed = allowed & (key_place <= place - base)
                value = jnp.where(allowed, value, -1e30)
                score_ref[i] = value
                tops = jnp.maximum(tops, value.reshape(tile // 8, 8, span).max(axis=0))
            top = jnp.max(tops, axis=0, keepdims=True) * EXP2_SCALE
            total = jnp.zeros((8, span), F32)
            out_t = jnp.zeros((HD, span), F32)
            for i, step in enumerate(steps):
                weight = jnp.exp2(score_ref[i] * EXP2_SCALE - top)
                score_ref[i] = weight
                out_t += jnp.dot(
                    value_turned[step], weight.astype(BF16), preferred_element_type=F32
                )
                total += weight.reshape(tile // 8, 8, span).sum(axis=0)
            inverse = 1.0 / jnp.sum(total, axis=0, keepdims=True)
            out_t = (out_t * inverse).astype(BF16).astype(F32)
            delta = jnp.sum(out_t * grad_t.astype(F32), axis=0, keepdims=True)
            put_queries(0, turn, out_t.T.astype(BF16))
            query_total = jnp.zeros((HD, span), F32)
            for i, step in enumerate(steps):
                prob = score_ref[i] * inverse
                value_sum[step] += jnp.dot(prob.astype(BF16), grad, preferred_element_type=F32)
                grad_prob = jnp.dot(keys_of(1, step), grad_t, preferred_element_type=F32)
                grad_score = (prob * (grad_prob - delta)).astype(BF16)
                key_sum[step] += jnp.dot(grad_score, query, preferred_element_type=F32)
                query_total += jnp.dot(
                    key_turned[step], grad_score, preferred_element_type=F32
                )
            put_queries(1, turn, (query_total * SCALE).T.astype(BF16))

        for count in range(1, score_ref.shape[0] + 1):

            @pl.when(last - first == count)
            def _():
                solve(count)

    @pl.loop(0, key_tiles)
    def _(step):
        at = pl.ds(pl.multiple_of(step * KR, KR), KR)
        for which, total, factor in ((0, key_sum, SCALE), (1, value_sum, 1.0)):
            for k, ref in enumerate(grad_refs):
                low = k * lanes * KR
                part = total[step, low : low + lanes * KR, :] * factor
                ref[:, which, at, :] = part.astype(ref.dtype).reshape(lanes, KR, HD)


def attend(head, query_parts, kv_parts, starts, begins, places, key_places):
    lanes, depth = len(query_parts), len(kv_parts)
    rows = query_parts[0].shape[1]
    turn_rows = query_rows(lanes)
    tile, span = depth * lanes * KR, lanes * GROUP * turn_rows
    key_tiles = rows // KR
    reach = turn_rows // KR + -(-(MOST - 1) // tile)
    vmem = pl.BlockSpec(memory_space=pltpu.VMEM)
    pairs = GROUP * rows * lanes * 640
    return pl.pallas_call(
        functools.partial(attend_kernel, head, lanes, depth),
        out_shape=[jax.ShapeDtypeStruct((2, rows, GROUP * HD), BF16)] * lanes
        + [
            jax.ShapeDtypeStruct(part.shape, F32 if k == 0 or (k == 2 and depth == 4) else BF16)
            for k, part in enumerate(kv_parts)
        ],
        in_specs=[pl.BlockSpec(memory_space=pltpu.SMEM)] + [vmem] * (3 + lanes + depth),
        out_specs=[vmem] * (lanes + depth),
        scratch_shapes=[
            pltpu.VMEM((key_tiles, HD, tile), BF16),
            pltpu.VMEM((key_tiles, HD, tile), BF16),
            pltpu.VMEM((key_tiles, tile, HD), F32),
            pltpu.VMEM((key_tiles, tile, HD), F32),
            pltpu.VMEM((min(reach, key_tiles), tile, span), F32),
            pltpu.VMEM((HD, span), F32),
            pltpu.VMEM((HD, span), F32),
        ],
        compiler_params=pltpu.CompilerParams(vmem_limit_bytes=(40 if depth == 4 else 62) << 20),
        cost_estimate=pl.CostEstimate(
            flops=80 * HD * pairs, bytes_accessed=8 << 20, transcendentals=pairs
        ),
    )(starts, begins, places, key_places, *query_parts, *kv_parts)


def moved(tensor, target):
    devices = lax.axis_size("seq")
    return lax.ppermute(tensor, "seq", [(i, target(i)) for i in range(devices)])


def swapped(tensor, mask):
    return moved(tensor, lambda i: i ^ mask)


def middle_swapped(tensor, lanes):
    return moved(tensor, lambda i: i if i // lanes in (0, 3) else i ^ (3 * lanes))


def outer_swapped(tensor, lanes):
    return moved(tensor, lambda i: i ^ (3 * lanes) if i // lanes in (0, 3) else i)


def after(tensor, *others):
    return lax.optimization_barrier((tensor, others))[0]


def plain_exchange(query_cuts, kv_owns, lanes, depth, run):
    heads = len(kv_owns)
    query_parts = [query_cuts[0]] + [swapped(query_cuts[mask], mask) for mask in range(1, lanes)]
    outs_back, totals = [], []
    for h in range(heads):
        own = kv_owns[h]
        outs, parts = run(
            h, query_parts, [own] + [swapped(own, k * lanes) for k in range(1, depth)]
        )
        outs_back.append([outs[0]] + [swapped(outs[mask], mask) for mask in range(1, lanes)])
        total = parts[0]
        for k in range(1, depth):
            total = total + swapped(parts[k].astype(BF16), k * lanes).astype(F32)
        totals.append(total.astype(BF16))
    return outs_back, totals


def ordered_exchange(query_cuts, kv_owns, lanes, inner, run):
    one, two, three = lanes, 2 * lanes, 3 * lanes
    query_x, query_d = swapped(query_cuts[2], 2), swapped(query_cuts[3], 3)
    a_two = swapped(kv_owns[0], two)
    a_one = swapped(kv_owns[0], one)
    a_three = middle_swapped(kv_owns[0], lanes)
    a_passed = swapped(a_two, one)
    b_three = middle_swapped(after(kv_owns[1], a_three, a_one, query_d), lanes)
    b_two = swapped(after(kv_owns[1], a_passed, b_three), two)
    b_far = outer_swapped(after(kv_owns[1], a_passed, b_three), lanes)
    b_one = swapped(after(kv_owns[1], query_x), one)
    query_c = swapped(after(query_cuts[1], query_d), 1)
    query_parts = [query_cuts[0], query_c, query_x, query_d]
    a_parts = [kv_owns[0], a_one, a_two, jnp.where(inner, a_three, a_passed)]
    def joined_two(parts, passed):
        return (parts[2] + jnp.where(inner, passed.astype(F32), 0.0)).astype(BF16)

    def total(parts, first, second, middle):
        value = parts[0] + first.astype(F32) + second.astype(F32)
        return (value + jnp.where(inner, middle.astype(F32), 0.0)).astype(BF16)

    outs_a, sum_a = run(0, query_parts, a_parts)
    b_three = jnp.where(inner, b_three, after(b_far, sum_a[0]))
    a_passed = swapped(sum_a[3], one)
    a_middle = middle_swapped(sum_a[3], lanes)
    a_two = swapped(joined_two(sum_a, a_passed), two)
    a_one = swapped(after(sum_a[1], b_far), one)
    out_ax = swapped(after(outs_a[2], b_one), 2)
    out_ad = swapped(after(outs_a[3], b_one), 3)
    outs_b, sum_b = run(
        1, query_parts, after([kv_owns[1], b_one, b_two, b_three], a_passed)
    )
    outs_b, sum_b = after((outs_b, sum_b), a_two, a_one, a_middle, out_ax, out_ad)
    b_passed = swapped(sum_b[3], one)
    out_ac = swapped(after(outs_a[1], a_one), 1)
    b_middle = middle_swapped(sum_b[3], lanes)
    out_bx = swapped(outs_b[2], 2)
    out_bd = swapped(outs_b[3], 3)
    b_send = joined_two(sum_b, b_passed)
    b_two = swapped(b_send, two)
    b_one = swapped(after(sum_b[1], b_send), one)
    out_bc = swapped(after(outs_b[1], out_bx), 1)
    totals = [
        after(total(sum_a, a_one, a_two, a_middle), out_bx),
        total(sum_b, b_one, b_two, b_middle),
    ]
    outs_back = [[outs_a[0], out_ac, out_ax, out_ad], [outs_b[0], out_bc, out_bx, out_bd]]
    return outs_back, totals


def on_device(queries, key_vectors, value_vectors, grad_output, document_ids):
    devices = lax.axis_size("seq")
    position = lax.axis_index("seq")
    rows = queries.shape[0]
    lanes = min(KV, devices // 4)
    depth = devices // lanes
    lane = position % lanes
    above = position - lane
    level = position // lanes
    inner = (level > 0) & (level < depth - 1)
    heads = KV // lanes
    wide, narrow = H * HD // lanes, KV * HD // lanes

    def cut(tensor, mask, width):
        return lax.dynamic_slice_in_dim(tensor, (lane ^ mask) * width, width, 1)

    def kv_cut(mask):
        both = jnp.stack([cut(key_vectors, mask, narrow), cut(value_vectors, mask, narrow)])
        return jnp.stack([both[:, :, h * HD : (h + 1) * HD] for h in range(heads)])

    def query_cut(mask):
        return jnp.stack([cut(queries, mask, wide), cut(grad_output, mask, wide)])

    kv_lanes = [kv_cut(0)] + [swapped(kv_cut(mask), mask) for mask in range(1, lanes)]
    queries, grad_output = (after(tensor, kv_lanes[1]) for tensor in (queries, grad_output))
    query_cuts = [query_cut(mask) for mask in range(lanes)]
    kv_owns = [jnp.stack([part[h] for part in kv_lanes]) for h in range(heads)]

    ids = document_ids.reshape(rows, devices)
    lane_masks = jnp.arange(lanes, dtype=jnp.int32)
    mine = above + (lane ^ lane_masks)
    column = jnp.arange(devices, dtype=jnp.int32)
    own_ids = jnp.sum(
        jnp.where(column[None, None, :] == mine[:, None, None], ids[None], 0), axis=-1
    )
    begin = jnp.sum(
        (document_ids[None, None, :] < own_ids[:, :, None]).astype(jnp.int32), axis=-1
    )
    place = jnp.arange(rows, dtype=jnp.int32)[None, :] * devices + mine[:, None]

    turn_rows = query_rows(lanes)

    def tiled(values):
        parts = values.reshape(lanes, rows // turn_rows, turn_rows).transpose(1, 0, 2)
        parts = parts.reshape(rows // turn_rows, 1, lanes * turn_rows)
        return jnp.tile(parts, (1, 1, GROUP))

    begins, places = tiled(begin), tiled(place)
    starts = jnp.min(begins, axis=(1, 2)) // (KR * devices)
    chunk = (jnp.arange(depth, dtype=jnp.int32) * lanes) ^ above
    key_place = (
        jnp.arange(KR, dtype=jnp.int32)[None, None, :] * devices
        + chunk[:, None, None]
        + (lane ^ lane_masks)[None, :, None]
    ).reshape(depth * lanes * KR, 1)
    key_places = jnp.broadcast_to(key_place, (depth * lanes * KR, 128))

    def run(h, query_parts, kv_parts):
        results = attend(h, query_parts, kv_parts, starts, begins, places, key_places)
        return results[:lanes], results[lanes:]

    if depth == 4 and lanes == 4 and heads == 2:
        outs_back, totals = ordered_exchange(query_cuts, kv_owns, lanes, inner, run)
    else:
        outs_back, totals = plain_exchange(query_cuts, kv_owns, lanes, depth, run)
    wholes = [jnp.zeros((rows, H * HD), BF16) for _ in range(2)]
    kv_wholes = [jnp.zeros((rows, KV * HD), BF16) for _ in range(2)]
    for h in range(heads):
        total = totals[h]
        kv_back = [total[0]] + [swapped(total[mask], mask) for mask in range(1, lanes)]
        for which in range(2):
            for mask in range(lanes):
                owner = lane ^ mask
                wholes[which] = lax.dynamic_update_slice_in_dim(
                    wholes[which], outs_back[h][mask][which], owner * wide + h * GROUP * HD, 1
                )
                kv_wholes[which] = lax.dynamic_update_slice_in_dim(
                    kv_wholes[which], kv_back[mask][which], owner * narrow + h * HD, 1
                )
    return (wholes[0], wholes[1], kv_wholes[0], kv_wholes[1])


def solution(mesh):
    placed = P(("group", "seq"), None)
    return jax.shard_map(
        on_device,
        mesh=mesh,
        in_specs=(placed, placed, placed, placed, P("group")),
        out_specs=(placed, placed, placed, placed),
        check_vma=False,
    )
```

```python
import functools
import math

import jax
import jax.numpy as jnp
from jax import lax
from jax.experimental import pallas as pl
from jax.experimental.pallas import tpu as pltpu
from jax.sharding import PartitionSpec as P

H = 32
KV = 8
HD = 128
MOST = 1024
GROUP = H // KV
KR = 16
F32 = jnp.float32
BF16 = jnp.bfloat16
SCALE = 1.0 / math.sqrt(HD)
EXP2_SCALE = SCALE * math.log2(math.e)


def query_rows(lanes):
    return max(16, 128 // lanes)


def attend_kernel(head, lanes, depth, start_ref, begin_ref, place_ref, key_place_ref, *refs):
    refs = list(refs)
    take = lambda count: [refs.pop(0) for _ in range(count)]
    query_refs, kv_refs = take(lanes), take(depth)
    out_refs, grad_refs = take(lanes), take(depth)
    key_turned, value_turned, key_sum, value_sum, score_ref, out_sum, query_sum = refs
    rows = query_refs[0].shape[1]
    turn_rows = query_rows(lanes)
    key_tiles, query_tiles = rows // KR, rows // turn_rows
    tile = depth * lanes * KR
    span = lanes * GROUP * turn_rows

    def keys_of(which, step):
        at = pl.ds(pl.multiple_of(step * KR, KR), KR)
        return jnp.concatenate(
            [ref[:, which, at, :].reshape(lanes * KR, HD) for ref in kv_refs], axis=0
        )

    def queries_of(which, step):
        at = pl.ds(pl.multiple_of(step * turn_rows, turn_rows), turn_rows)
        return jnp.concatenate(
            [
                ref[which, at, (head * GROUP + j) * HD : (head * GROUP + j + 1) * HD]
                for j in range(GROUP)
                for ref in query_refs
            ],
            axis=0,
        )

    def put_queries(which, step, value):
        at = pl.ds(pl.multiple_of(step * turn_rows, turn_rows), turn_rows)
        for j in range(GROUP):
            for lane, ref in enumerate(out_refs):
                low = (j * lanes + lane) * turn_rows
                ref[which, at, j * HD : (j + 1) * HD] = value[low : low + turn_rows]

    @pl.loop(0, key_tiles)
    def _(step):
        key_turned[step] = keys_of(0, step).T
        value_turned[step] = keys_of(1, step).T
        key_sum[step] = jnp.zeros((tile, HD), F32)
        value_sum[step] = jnp.zeros((tile, HD), F32)

    @pl.loop(0, query_tiles)
    def _(turn):
        query, grad = queries_of(0, turn), queries_of(1, turn)
        query_t, grad_t = query.T, grad.T
        first = start_ref[turn]
        last = (turn + 1) * (turn_rows // KR)
        begin, place = begin_ref[turn], place_ref[turn]

        def solve(count):
            tops = jnp.full((8, span), -1e30, F32)
            steps = [last - count + i for i in range(count)]
            key_place = jnp.concatenate([key_place_ref[...]] * (span // 128), axis=1)
            for i, step in enumerate(steps):
                base = step * tile
                value = jnp.dot(keys_of(0, step), query_t, preferred_element_type=F32)
                allowed = key_place >= begin - base
                if i >= count - turn_rows // KR:
                    allowed = allowed & (key_place <= place - base)
                value = jnp.where(allowed, value, -1e30)
                score_ref[i] = value
                tops = jnp.maximum(tops, value.reshape(tile // 8, 8, span).max(axis=0))
            top = jnp.max(tops, axis=0, keepdims=True) * EXP2_SCALE
            total = jnp.zeros((8, span), F32)
            out_t = jnp.zeros((HD, span), F32)
            for i, step in enumerate(steps):
                weight = jnp.exp2(score_ref[i] * EXP2_SCALE - top)
                score_ref[i] = weight
                out_t += jnp.dot(
                    value_turned[step], weight.astype(BF16), preferred_element_type=F32
                )
                total += weight.reshape(tile // 8, 8, span).sum(axis=0)
            inverse = 1.0 / jnp.sum(total, axis=0, keepdims=True)
            out_t = (out_t * inverse).astype(BF16).astype(F32)
            delta = jnp.sum(out_t * grad_t.astype(F32), axis=0, keepdims=True)
            put_queries(0, turn, out_t.T.astype(BF16))
            query_total = jnp.zeros((HD, span), F32)
            for i, step in enumerate(steps):
                prob = score_ref[i] * inverse
                value_sum[step] += jnp.dot(prob.astype(BF16), grad, preferred_element_type=F32)
                grad_prob = jnp.dot(keys_of(1, step), grad_t, preferred_element_type=F32)
                grad_score = (prob * (grad_prob - delta)).astype(BF16)
                key_sum[step] += jnp.dot(grad_score, query, preferred_element_type=F32)
                query_total += jnp.dot(
                    key_turned[step], grad_score, preferred_element_type=F32
                )
            put_queries(1, turn, (query_total * SCALE).T.astype(BF16))

        for count in range(1, score_ref.shape[0] + 1):

            @pl.when(last - first == count)
            def _():
                solve(count)

    @pl.loop(0, key_tiles)
    def _(step):
        at = pl.ds(pl.multiple_of(step * KR, KR), KR)
        for which, total, factor in ((0, key_sum, SCALE), (1, value_sum, 1.0)):
            for k, ref in enumerate(grad_refs):
                low = k * lanes * KR
                part = total[step, low : low + lanes * KR, :] * factor
                ref[:, which, at, :] = part.astype(ref.dtype).reshape(lanes, KR, HD)


def attend(head, query_parts, kv_parts, starts, begins, places, key_places):
    lanes, depth = len(query_parts), len(kv_parts)
    rows = query_parts[0].shape[1]
    turn_rows = query_rows(lanes)
    tile, span = depth * lanes * KR, lanes * GROUP * turn_rows
    key_tiles = rows // KR
    reach = turn_rows // KR + -(-(MOST - 1) // tile)
    vmem = pl.BlockSpec(memory_space=pltpu.VMEM)
    pairs = GROUP * rows * lanes * 640
    return pl.pallas_call(
        functools.partial(attend_kernel, head, lanes, depth),
        out_shape=[jax.ShapeDtypeStruct((2, rows, GROUP * HD), BF16)] * lanes
        + [
            jax.ShapeDtypeStruct(part.shape, F32 if k == 0 or (k == 2 and depth == 4) else BF16)
            for k, part in enumerate(kv_parts)
        ],
        in_specs=[pl.BlockSpec(memory_space=pltpu.SMEM)] + [vmem] * (3 + lanes + depth),
        out_specs=[vmem] * (lanes + depth),
        scratch_shapes=[
            pltpu.VMEM((key_tiles, HD, tile), BF16),
            pltpu.VMEM((key_tiles, HD, tile), BF16),
            pltpu.VMEM((key_tiles, tile, HD), F32),
            pltpu.VMEM((key_tiles, tile, HD), F32),
            pltpu.VMEM((min(reach, key_tiles), tile, span), F32),
            pltpu.VMEM((HD, span), F32),
            pltpu.VMEM((HD, span), F32),
        ],
        compiler_params=pltpu.CompilerParams(vmem_limit_bytes=(40 if depth == 4 else 62) << 20),
        cost_estimate=pl.CostEstimate(
            flops=80 * HD * pairs, bytes_accessed=8 << 20, transcendentals=pairs
        ),
    )(starts, begins, places, key_places, *query_parts, *kv_parts)


def moved(tensor, target):
    devices = lax.axis_size("seq")
    return lax.ppermute(tensor, "seq", [(i, target(i)) for i in range(devices)])


def swapped(tensor, mask):
    return moved(tensor, lambda i: i ^ mask)


def middle_swapped(tensor, lanes):
    return moved(tensor, lambda i: i if i // lanes in (0, 3) else i ^ (3 * lanes))


def outer_swapped(tensor, lanes):
    return moved(tensor, lambda i: i ^ (3 * lanes) if i // lanes in (0, 3) else i)


def after(tensor, *others):
    return lax.optimization_barrier((tensor, others))[0]


def plain_exchange(query_cuts, kv_owns, lanes, depth, run):
    heads = len(kv_owns)
    query_parts = [query_cuts[0]] + [swapped(query_cuts[mask], mask) for mask in range(1, lanes)]
    outs_back, totals = [], []
    for h in range(heads):
        own = kv_owns[h]
        outs, parts = run(
            h, query_parts, [own] + [swapped(own, k * lanes) for k in range(1, depth)]
        )
        outs_back.append([outs[0]] + [swapped(outs[mask], mask) for mask in range(1, lanes)])
        total = parts[0]
        for k in range(1, depth):
            total = total + swapped(parts[k].astype(BF16), k * lanes).astype(F32)
        totals.append(total.astype(BF16))
    return outs_back, totals


def ordered_exchange(query_cuts, kv_owns, lanes, inner, run):
    one, two, three = lanes, 2 * lanes, 3 * lanes
    query_x, query_d = swapped(query_cuts[2], 2), swapped(query_cuts[3], 3)
    a_two = swapped(kv_owns[0], two)
    a_one = swapped(kv_owns[0], one)
    a_three = middle_swapped(kv_owns[0], lanes)
    a_passed = swapped(a_two, one)
    b_three = middle_swapped(after(kv_owns[1], a_three, a_one, query_d), lanes)
    b_two = swapped(after(kv_owns[1], a_passed), two)
    b_far = outer_swapped(after(kv_owns[1], a_passed), lanes)
    b_one = swapped(after(kv_owns[1], query_x), one)
    query_c = swapped(after(query_cuts[1], query_d), 1)
    query_parts = [query_cuts[0], query_c, query_x, query_d]
    a_parts = [kv_owns[0], a_one, a_two, jnp.where(inner, a_three, a_passed)]
    def joined_two(parts, passed):
        return (parts[2] + jnp.where(inner, passed.astype(F32), 0.0)).astype(BF16)

    def total(parts, first, second, middle):
        value = parts[0] + first.astype(F32) + second.astype(F32)
        return (value + jnp.where(inner, middle.astype(F32), 0.0)).astype(BF16)

    outs_a, sum_a = run(0, query_parts, a_parts)
    b_three = jnp.where(inner, b_three, after(b_far, sum_a[0]))
    a_passed = swapped(sum_a[3], one)
    a_middle = middle_swapped(sum_a[3], lanes)
    a_two = swapped(joined_two(sum_a, a_passed), two)
    a_one = swapped(after(sum_a[1], b_far), one)
    out_ax = swapped(after(outs_a[2], b_one), 2)
    out_ad = swapped(after(outs_a[3], b_one), 3)
    outs_b, sum_b = run(
        1, query_parts, after([kv_owns[1], b_one, b_two, b_three], a_passed)
    )
    outs_b, sum_b = after((outs_b, sum_b), a_two, a_one, a_middle, out_ax, out_ad)
    b_passed = swapped(sum_b[3], one)
    out_ac = swapped(after(outs_a[1], a_one), 1)
    b_middle = middle_swapped(sum_b[3], lanes)
    out_bx = swapped(outs_b[2], 2)
    out_bd = swapped(outs_b[3], 3)
    b_send = joined_two(sum_b, b_passed)
    b_two = swapped(b_send, two)
    b_one = swapped(after(sum_b[1], b_send), one)
    out_bc = swapped(after(outs_b[1], out_bx), 1)
    totals = [
        after(total(sum_a, a_one, a_two, a_middle), out_bx),
        total(sum_b, b_one, b_two, b_middle),
    ]
    outs_back = [[outs_a[0], out_ac, out_ax, out_ad], [outs_b[0], out_bc, out_bx, out_bd]]
    return outs_back, totals


def on_device(queries, key_vectors, value_vectors, grad_output, document_ids):
    devices = lax.axis_size("seq")
    position = lax.axis_index("seq")
    rows = queries.shape[0]
    lanes = min(KV, devices // 4)
    depth = devices // lanes
    lane = position % lanes
    above = position - lane
    level = position // lanes
    inner = (level > 0) & (level < depth - 1)
    heads = KV // lanes
    wide, narrow = H * HD // lanes, KV * HD // lanes

    def cut(tensor, mask, width):
        return lax.dynamic_slice_in_dim(tensor, (lane ^ mask) * width, width, 1)

    def kv_cut(mask):
        both = jnp.stack([cut(key_vectors, mask, narrow), cut(value_vectors, mask, narrow)])
        return jnp.stack([both[:, :, h * HD : (h + 1) * HD] for h in range(heads)])

    def query_cut(mask):
        return jnp.stack([cut(queries, mask, wide), cut(grad_output, mask, wide)])

    kv_lanes = [kv_cut(0)] + [swapped(kv_cut(mask), mask) for mask in range(1, lanes)]
    queries, grad_output = (after(tensor, kv_lanes[1]) for tensor in (queries, grad_output))
    query_cuts = [query_cut(mask) for mask in range(lanes)]
    kv_owns = [jnp.stack([part[h] for part in kv_lanes]) for h in range(heads)]

    ids = document_ids.reshape(rows, devices)
    lane_masks = jnp.arange(lanes, dtype=jnp.int32)
    mine = above + (lane ^ lane_masks)
    column = jnp.arange(devices, dtype=jnp.int32)
    own_ids = jnp.sum(
        jnp.where(column[None, None, :] == mine[:, None, None], ids[None], 0), axis=-1
    )
    begin = jnp.sum(
        (document_ids[None, None, :] < own_ids[:, :, None]).astype(jnp.int32), axis=-1
    )
    place = jnp.arange(rows, dtype=jnp.int32)[None, :] * devices + mine[:, None]

    turn_rows = query_rows(lanes)

    def tiled(values):
        parts = values.reshape(lanes, rows // turn_rows, turn_rows).transpose(1, 0, 2)
        parts = parts.reshape(rows // turn_rows, 1, lanes * turn_rows)
        return jnp.tile(parts, (1, 1, GROUP))

    begins, places = tiled(begin), tiled(place)
    starts = jnp.min(begins, axis=(1, 2)) // (KR * devices)
    chunk = (jnp.arange(depth, dtype=jnp.int32) * lanes) ^ above
    key_place = (
        jnp.arange(KR, dtype=jnp.int32)[None, None, :] * devices
        + chunk[:, None, None]
        + (lane ^ lane_masks)[None, :, None]
    ).reshape(depth * lanes * KR, 1)
    key_places = jnp.broadcast_to(key_place, (depth * lanes * KR, 128))

    def run(h, query_parts, kv_parts):
        results = attend(h, query_parts, kv_parts, starts, begins, places, key_places)
        return results[:lanes], results[lanes:]

    if depth == 4 and lanes == 4 and heads == 2:
        outs_back, totals = ordered_exchange(query_cuts, kv_owns, lanes, inner, run)
    else:
        outs_back, totals = plain_exchange(query_cuts, kv_owns, lanes, depth, run)
    wholes = [jnp.zeros((rows, H * HD), BF16) for _ in range(2)]
    kv_wholes = [jnp.zeros((rows, KV * HD), BF16) for _ in range(2)]
    for h in range(heads):
        total = totals[h]
        kv_back = [total[0]] + [swapped(total[mask], mask) for mask in range(1, lanes)]
        for which in range(2):
            for mask in range(lanes):
                owner = lane ^ mask
                wholes[which] = lax.dynamic_update_slice_in_dim(
                    wholes[which], outs_back[h][mask][which], owner * wide + h * GROUP * HD, 1
                )
                kv_wholes[which] = lax.dynamic_update_slice_in_dim(
                    kv_wholes[which], kv_back[mask][which], owner * narrow + h * HD, 1
                )
    return (wholes[0], wholes[1], kv_wholes[0], kv_wholes[1])


def solution(mesh):
    placed = P(("group", "seq"), None)
    return jax.shard_map(
        on_device,
        mesh=mesh,
        in_specs=(placed, placed, placed, placed, P("group")),
        out_specs=(placed, placed, placed, placed),
        check_vma=False,
    )
```
